32 devices in a mesh: dp: 4 (over y, core), expert: 8 (over z, x).
Axes of the slice: x: 2, y: 2, z: 4, core: 2. Of those that a mesh axis runs over, the one named last changes fastest.
Arguments:
- tokens: bfloat16 [4096, 2048], P(('dp', 'expert')), may hold values from -6 to 6
- out_grad: bfloat16 [4096, 2048], P(('dp', 'expert')), may hold values from -3 to 3
- expert_ids: int32 [4096, 8], P(('dp', 'expert')), may hold values from 0 to 15, all different within a row; in each aligned block of 128 rows (0 to 127, 128 to 255, ...) at most 68 rows name the same one
- gate_probs: bfloat16 [4096, 8], P(('dp', 'expert')), may hold values from 0.019897461 to 0.3984375
- gate_up_weight: bfloat16 [16, 2048, 768], P('expert'), may hold values from -0.125 to 0.125
- down_weight: bfloat16 [16, 384, 2048], P('expert'), may hold values from -0.3125 to 0.3125
Outputs:
- grad_tokens: bfloat16 [4096, 2048], P(('dp', 'expert'))
- grad_probs: bfloat16 [4096, 8], P(('dp', 'expert'))
- grad_weights: bfloat16 [2048, 16, 1152], P('dp', 'expert')
The draws below stay inside these ranges and needn't reach their ends.
Inputs may be any that keep to these rules, and one draw needn't show every extreme that they name: `expert_ids`: each row names 8 distinct experts; in each aligned block of 128 rows no expert is named by more than 68 rows.
All inputs are finite; a program needn't handle non-finite values.
Results may differ from the reference program's by a relative error of at most 0.013.
Values may be sent and summed in bfloat16 or wider, within the bound.
No kernel may reach another device: no remote copies, remote signals or barrier semaphores. Data moves between devices by JAX's collectives and lax.ppermute only.
A program may use at most 128 MiB of HBM per device.

```python
import math
import jax
import jax.numpy as jnp
import numpy as np
from jax import lax

D = 2048
FF = 384
TOP = 8
TOK_DEV = 128
EXPERTS = 16
MOST = 68
TOKENS = 4096
N_DP = 4
N_EXPERT = 8


def block_scale(stream_key, dims, shards, smallest, high):
    loudness, own = 1.0, jax.random.fold_in(stream_key, 6)
    for dim, blocks in shards:
        draws = jnp.exp(jax.random.uniform(jax.random.fold_in(own, dim), (blocks,), jnp.float32, smallest / len(shards), high / len(shards)))
        loudness = loudness * jnp.repeat(draws, dims[dim] // blocks).reshape([-1 if axis == dim else 1 for axis in range(len(dims))])
    return loudness


def shared_out(own_key, own, number, rows, number_of, top, most, skew):
    order = jax.random.permutation(own_key, number_of)
    heavy_load, common = portions_of(number_of, rows * top, most, skew, True), portions_of(number_of, rows * top, most, skew, False)
    places = jnp.arange(number_of)

    def named(lengths, offset_by):
        used = int((lengths > 0).sum())
        fixed = max(1, used // 4)
        moved = fixed + (places - fixed + offset_by * (used - fixed)) % max(1, number_of - fixed)
        return jnp.zeros((number_of,), jnp.int32).at[order[jnp.where(places < fixed, places, moved)]].set(jnp.asarray(lengths, jnp.int32))

    lengths = jnp.where(number % 4 == 0, named(heavy_load, number // 4), named(common, number - number // 4 - 1))
    mixed = jax.random.permutation(jax.random.fold_in(own, 3), number_of)
    giver, sink = mixed[0:number_of // 2 * 2:2], mixed[1:number_of // 2 * 2:2]
    room = jnp.minimum(lengths[giver] - 1, most - lengths[sink]) // 2
    room = jnp.where((giver == order[0]) | (sink == order[0]) | (lengths[sink] == 0), 0, jnp.maximum(room, 0))
    moved = jax.random.randint(jax.random.fold_in(own, 4), (number_of // 2,), 0, 1 << 20) % (room + 1)
    lengths = lengths.at[giver].add(-moved).at[sink].add(moved)
    items = jnp.searchsorted(jnp.cumsum(lengths), jnp.arange(rows * top), side="right").astype(jnp.int32)
    grid = items.reshape(top, rows).T
    grid = grid[jax.random.permutation(jax.random.fold_in(own, 1), rows)]
    offset_by = jax.random.randint(jax.random.fold_in(own, 2), (rows, 1), 0, top)
    return jnp.take_along_axis(grid, (jnp.arange(top)[None, :] + offset_by) % top, axis=1)


def portions_of(number_of, total, bound, skew, full):
    loads = [(1 << 20) // math.isqrt(rank ** skew) + 1 for rank in range(1, number_of + 1)]
    largest = bound if full else min(bound, max(-(-total // number_of), total * loads[0] // sum(loads)))
    least = 1 if total - largest >= number_of - 1 else 0
    holding, rest = [largest] + [least] * (number_of - 1), total - largest - least * (number_of - 1)
    while rest > 0:
        free = [i for i in range(1, number_of) if holding[i] < largest] or [i for i in range(1, number_of) if holding[i] < bound]
        mass, left = sum([loads[i] for i in free]), rest
        for i in free:
            more = min(bound - holding[i], max(1, left * loads[i] // mass), rest)
            holding[i] = holding[i] + more
            rest = rest - more
    return np.array(holding)


def centred(key, dims, spread, reach, split=(), kind=jnp.bfloat16):
    array = jax.random.normal(key, dims, jnp.float32) * spread
    if len(split) > 0:
        array = block_scale(key, dims, split, -0.22, 0.18) * array
    return jnp.clip(array, min=-reach, max=reach).astype(kind)


def setup_inputs(seed: int = 0) -> dict:
    streams_of = jax.random.split(jax.random.key(seed), 7)
    tokens = centred(streams_of[0], (TOKENS, D), 1.0, 6.0, ((0, 32),))
    out_grad = centred(streams_of[1], (TOKENS, D), 0.5, 3.0, ((0, 32),))
    expert_ids_keys = jax.random.split(jax.random.fold_in(streams_of[2], 1), TOKENS // TOK_DEV)
    expert_ids_turns = jax.random.permutation(jax.random.fold_in(streams_of[2], 3), TOKENS // TOK_DEV)
    expert_ids = jax.vmap(lambda own, number: shared_out(jax.random.fold_in(streams_of[2], 2), own, number, TOK_DEV, EXPERTS, TOP, MOST, 2))(expert_ids_keys, expert_ids_turns).reshape((TOKENS, TOP))
    gate_probs = jnp.clip(jnp.exp(math.log(0.3984375) - 2.9969585 * jax.random.uniform(streams_of[3], (TOKENS, TOP), jnp.float32) ** block_scale(streams_of[3], (TOKENS, TOP), ((0, 32),), -0.2, 0.2)), 0.019897461, 0.3984375).astype(jnp.bfloat16)
    gate_up_weight = centred(streams_of[4], (EXPERTS, D, 2 * FF), D ** -0.5, 0.125, ((0, 8),))
    down_weight = centred(streams_of[5], (EXPERTS, FF, D), FF ** -0.5, 0.3125, ((0, 8),))
    return dict(tokens=tokens, out_grad=out_grad, expert_ids=expert_ids, gate_probs=gate_probs, gate_up_weight=gate_up_weight, down_weight=down_weight)


def rounded(value):
    return lax.optimization_barrier(value.astype(jnp.bfloat16)).astype(jnp.float32)


def silu_parts(gate_pre):
    logistic = jax.nn.sigmoid(gate_pre)
    return gate_pre * logistic, logistic * (1.0 + gate_pre * (1.0 - logistic))


def reference(tokens, out_grad, expert_ids, gate_probs, gate_up_weight, down_weight):
    token_count = tokens.shape[0]
    blocks = token_count // TOK_DEV
    pair_count = token_count * TOP
    block_ids = expert_ids.reshape(blocks, TOK_DEV * TOP)
    onehot = (block_ids[:, :, None] == jnp.arange(EXPERTS, dtype=jnp.int32)[None, None, :]).astype(jnp.int32)
    ranking = jnp.sum((jnp.cumsum(onehot, axis=1) - onehot) * onehot, axis=2)
    block_index = jnp.arange(blocks, dtype=jnp.int32)[:, None]
    placement = (block_ids * blocks + block_index) * MOST + ranking
    slot_table = jnp.full((EXPERTS * blocks * MOST,), pair_count, jnp.int32)
    slot_table = slot_table.at[placement.reshape(-1)].set(jnp.arange(pair_count, dtype=jnp.int32))
    slot_table = slot_table.reshape(EXPERTS, blocks * MOST)
    flat_probs = gate_probs.reshape(-1)

    def one_expert(carry, inputs):
        grad_rows, grad_gate = carry
        slot_index, weight_in, weight_out = inputs
        filled = slot_index < pair_count
        clipped = jnp.minimum(slot_index, pair_count - 1)
        owner_token = clipped // TOP
        inputs_rows = jnp.where(filled[:, None], tokens[owner_token], 0).astype(jnp.float32)
        cotangent = jnp.where(filled[:, None], out_grad[owner_token], 0).astype(jnp.float32)
        weights_rows = jnp.where(filled, flat_probs[clipped], 0).astype(jnp.float32)
        weight_in32 = weight_in.astype(jnp.float32)
        weight_out32 = weight_out.astype(jnp.float32)
        pre_acts = jnp.dot(inputs_rows, weight_in32, preferred_element_type=jnp.float32)
        gate_pre = pre_acts[:, :FF]
        up_pre = pre_acts[:, FF:]
        active, slope_terms = silu_parts(gate_pre)
        hidden = rounded(active * up_pre)
        expert_out = jnp.dot(hidden, weight_out32, preferred_element_type=jnp.float32)
        gate_grad = jnp.sum(cotangent * expert_out, axis=1).astype(jnp.bfloat16)
        scaled = rounded(weights_rows[:, None] * cotangent)
        grad_hidden = jnp.dot(scaled, weight_out32.T, preferred_element_type=jnp.float32)
        grad_pre = rounded(jnp.concatenate([grad_hidden * up_pre * slope_terms, grad_hidden * active], axis=1))
        row_grad = rounded(jnp.dot(grad_pre, weight_in32.T, preferred_element_type=jnp.float32))
        grad_rows = grad_rows.at[jnp.where(filled, owner_token, token_count)].add(row_grad, mode="drop")
        grad_gate = grad_gate.at[slot_index].set(gate_grad, mode="drop")
        inputs_dp = inputs_rows.reshape(N_DP, N_EXPERT * MOST, D)
        pre_dp = grad_pre.reshape(N_DP, N_EXPERT * MOST, 2 * FF)
        scaled_dp = scaled.reshape(N_DP, N_EXPERT * MOST, D)
        hidden_dp = hidden.reshape(N_DP, N_EXPERT * MOST, FF)
        part_in = jnp.einsum("prd,prf->pdf", inputs_dp, pre_dp)
        part_out = jnp.einsum("prd,prf->pdf", scaled_dp, hidden_dp)
        partial_value = rounded(jnp.concatenate([part_in, part_out], axis=2))
        summed = jnp.sum(partial_value, axis=0).astype(jnp.bfloat16)
        return (grad_rows, grad_gate), summed

    start_rows = jnp.zeros((token_count, D), jnp.float32)
    start_gate = jnp.zeros((pair_count,), jnp.bfloat16)
    (grad_rows, grad_gate), stacked = lax.scan(one_expert, (start_rows, start_gate), (slot_table, gate_up_weight, down_weight))
    grad_weights = jnp.transpose(stacked, (1, 0, 2))
    return grad_rows.astype(jnp.bfloat16), grad_gate.reshape(token_count, TOP), grad_weights
```

```python
import functools

import jax
import jax.numpy as jnp
from jax import lax
from jax.experimental import pallas as pl
from jax.experimental.pallas import tpu as pltpu
from jax.sharding import PartitionSpec as P


def ring_order(size):
    half = size // 2
    return [2 * p if p < half else 2 * (size - 1 - p) + 1 for p in range(size)]


def joined(refs):
    parts = [ref[...] for ref in refs]
    return parts[0] if len(parts) == 1 else jnp.concatenate(parts, axis=0)


def expert_kernel(count, _, *refs):
    x_refs, g_refs, gate_refs = refs[:count], refs[count : 2 * count], refs[2 * count : 3 * count]
    w_in, w_out, probs_ref, pre_ref, hidden_ref = refs[3 * count : 3 * count + 5]
    row_refs, total = refs[3 * count + 5 : -1], refs[-1]
    e, last = pl.program_id(0), pl.num_programs(0) - 1
    units = w_out.shape[1]
    pre = jnp.dot(joined(x_refs), w_in[0], preferred_element_type=jnp.float32)
    back = lax.dot_general(
        joined(g_refs), w_out[0], (((1,), (1,)), ((), ())), preferred_element_type=jnp.float32
    )
    gates = [ref[0].astype(jnp.float32) for ref in gate_refs]
    gates = gates[0] if count == 1 else jnp.concatenate(gates, axis=0)
    column = lax.broadcasted_iota(jnp.int32, gates.shape, 1) == e
    weight = jnp.sum(jnp.where(column, gates, 0.0), axis=1, keepdims=True)
    gate_pre, up_pre = pre[:, :units], pre[:, units:]
    logistic = 1.0 / (1.0 + jnp.exp(-gate_pre))
    active = gate_pre * logistic
    slope = logistic * (1.0 + gate_pre * (1.0 - logistic))
    hidden = (active * up_pre).astype(jnp.bfloat16).astype(jnp.float32)
    probs = jnp.sum(hidden * back, axis=1, keepdims=True)
    probs_ref[...] = jnp.where(column, probs, probs_ref[...])
    hidden_ref[0] = (weight * hidden).astype(jnp.bfloat16)
    grad_hidden = weight * back
    pre_ref[0, :, :units] = (grad_hidden * up_pre * slope).astype(jnp.bfloat16)
    pre_ref[0, :, units:] = (grad_hidden * active).astype(jnp.bfloat16)
    rows = lax.dot_general(
        pre_ref[0], w_in[0], (((1,), (1,)), ((), ())), preferred_element_type=jnp.float32
    )

    @pl.when(e == 0)
    def _():
        total[...] = rows

    @pl.when(e > 0)
    def _():
        total[...] += rows

    @pl.when(e == last)
    def _():
        at = 0
        for ref in row_refs:
            ref[...] = total[at : at + ref.shape[0]].astype(jnp.bfloat16)
            at += ref.shape[0]


def expert_blocks(blocks, sources, gates, weight_in, weight_out):
    count = len(blocks)
    experts, width, wide = weight_in.shape
    units = weight_out.shape[1]
    sizes = [hi - lo for lo, hi, _, _ in blocks]
    rows = sum(sizes)
    whole = lambda n: pl.BlockSpec((n, width), lambda e, s: (0, 0))

    def gate_spec(i, lo, n):
        return pl.BlockSpec((1, n, experts), lambda e, s: (s[i], lo // n, 0))

    per_expert = lambda a, b: pl.BlockSpec((1, a, b), lambda e, s: (e, 0, 0))
    out = pl.pallas_call(
        functools.partial(expert_kernel, count),
        out_shape=[
            jax.ShapeDtypeStruct((rows, experts), jnp.float32),
            jax.ShapeDtypeStruct((experts, rows, wide), jnp.bfloat16),
            jax.ShapeDtypeStruct((experts, rows, units), jnp.bfloat16),
        ]
        + [jax.ShapeDtypeStruct((n, width), jnp.bfloat16) for n in sizes],
        grid_spec=pltpu.PrefetchScalarGridSpec(
            num_scalar_prefetch=1,
            grid=(experts,),
            in_specs=[whole(n) for n in sizes] * 2
            + [gate_spec(i, blocks[i][0], sizes[i]) for i in range(count)]
            + [per_expert(width, wide), per_expert(units, width)],
            out_specs=[
                pl.BlockSpec((rows, experts), lambda e, s: (0, 0)),
                per_expert(rows, wide),
                per_expert(rows, units),
            ]
            + [whole(n) for n in sizes],
            scratch_shapes=[pltpu.VMEM((rows, width), jnp.float32)],
        ),
        cost_estimate=pl.CostEstimate(
            flops=2 * rows * experts * width * (2 * wide + units),
            bytes_accessed=2 * experts * width * (wide + units) + 8 * rows * width,
            transcendentals=0,
        ),
        name="experts",
    )(
        jnp.stack(sources).astype(jnp.int32),
        *[b[2] for b in blocks],
        *[b[3] for b in blocks],
        *[gates] * count,
        weight_in,
        weight_out,
    )
    return out[0], out[1], out[2], out[3:]


def outer_product(x_refs, p_refs):
    left = joined(x_refs)
    right = [jnp.concatenate([ref[k] for ref in p_refs], axis=0) for k in range(p_refs[0].shape[0])]
    return [
        lax.dot_general(left, r, (((0,), (0,)), ((), ())), preferred_element_type=jnp.float32)
        for r in right
    ]


def sent_kernel(nx, np_, _, *refs):
    out = refs[-1]
    at = 0
    for part in outer_product(refs[:nx], refs[nx : nx + np_]):
        out[0, :, at : at + part.shape[1]] = part.astype(jnp.bfloat16)
        at += part.shape[1]


def kept_kernel(nx, np_, _, *refs):
    arrived, sent, own = refs[nx + np_ :]
    step, last = pl.program_id(0), pl.num_programs(0) - 1
    at = 0
    for part in outer_product(refs[:nx], refs[nx : nx + np_]):
        span = slice(at, at + part.shape[1])
        part = (part + arrived[0, :, span].astype(jnp.float32)).astype(jnp.bfloat16)

        @pl.when(step < last)
        def _():
            sent[0, :, span] = part

        @pl.when(step == last)
        def _():
            own[:, span] = part

        at += part.shape[1]


def weight_part(xs, ps, expert, where, replicas, arrived=None):
    width = xs[0].shape[1]
    outer, depth = replicas // 2, width // replicas
    picked = 1 if expert is not None else ps[0].shape[0]
    first = expert if expert is not None else 0
    columns = picked * ps[0].shape[2]
    if arrived is None:
        block = lambda i, s: 2 * i + 1 - s[0]
    else:
        block = lambda i, s: 2 * ((s[1] + 1 + i) % outer) + s[0]
    in_specs = [pl.BlockSpec((x.shape[0], depth), lambda i, s: (0, block(i, s))) for x in xs]
    in_specs += [
        pl.BlockSpec((picked,) + p.shape[1:], lambda i, s: (first // picked, 0, 0)) for p in ps
    ]
    total_rows = sum(x.shape[0] for x in xs)
    cost = pl.CostEstimate(
        flops=2 * total_rows * outer * depth * columns,
        bytes_accessed=2 * (total_rows * (outer * depth + columns) + outer * depth * columns),
        transcendentals=0,
    )
    piece = (1, depth, columns)
    if arrived is None:
        kernel, args = sent_kernel, ()
        out_shape = jax.ShapeDtypeStruct((outer, depth, columns), jnp.bfloat16)
        out_specs = pl.BlockSpec(piece, lambda i, s: (i, 0, 0))
    else:
        kernel, args = kept_kernel, (arrived,)
        in_specs.append(pl.BlockSpec(piece, lambda i, s: ((s[1] + 1 + i) % outer, 0, 0)))
        out_shape = [
            jax.ShapeDtypeStruct((outer - 1, depth, columns), jnp.bfloat16),
            jax.ShapeDtypeStruct((depth, columns), jnp.bfloat16),
        ]
        out_specs = [
            pl.BlockSpec(piece, lambda i, s: (jnp.minimum(i, outer - 2), 0, 0)),
            pl.BlockSpec((depth, columns), lambda i, s: (0, 0)),
        ]
    return pl.pallas_call(
        functools.partial(kernel, len(xs), len(ps)),
        out_shape=out_shape,
        grid_spec=pltpu.PrefetchScalarGridSpec(
            num_scalar_prefetch=1, grid=(outer,), in_specs=in_specs, out_specs=out_specs
        ),
        cost_estimate=cost,
        name="weights_sent" if arrived is None else "weights_kept",
    )(where, *xs, *ps, *args)


def on_device(tokens, out_grad, expert_ids, gate_probs, gate_up_weight, down_weight):
    rows, width = tokens.shape
    local_experts = gate_up_weight.shape[0]
    size = lax.axis_size("expert")
    expert_count = local_experts * size
    half, mid = size // 2, rows // 2
    order = ring_order(size)
    forward = [(order[p], order[(p + 1) % size]) for p in range(size)]
    backward = [(b, a) for a, b in forward]
    me = lax.axis_index("expert")
    place = jnp.where(me % 2 == 0, me // 2, size - 1 - me // 2)

    experts = jnp.arange(expert_count, dtype=jnp.int32)
    onehot = expert_ids[:, :, None] == experts[None, None, :]
    dense_gates = jnp.sum(
        jnp.where(onehot, gate_probs[:, :, None].astype(jnp.float32), 0.0), axis=1
    ).astype(jnp.bfloat16)
    gates = lax.all_to_all(dense_gates, "expert", split_axis=1, concat_axis=0, tiled=True)
    gates = gates.reshape(size, rows, local_experts)
    ring = jnp.asarray(order, jnp.int32)
    source = lambda offset: ring[(place + offset) % size]

    blocks = [(0, 0, rows, tokens, out_grad)]
    left, right = (tokens, out_grad), (tokens, out_grad)
    for step in range(1, half):
        left = tuple(lax.ppermute(a, "expert", forward) for a in left)
        right = tuple(lax.ppermute(a, "expert", backward) for a in right)
        blocks.append((size - step, 0, rows) + left)
        blocks.append((step, 0, rows) + right)
    left = tuple(lax.ppermute(a[:mid], "expert", forward) for a in left)
    right = tuple(lax.ppermute(a[mid:], "expert", backward) for a in right)
    blocks.append((half, 0, mid) + left)
    blocks.append((half, mid, rows) + right)

    groups = [blocks[:1]] + [blocks[i : i + 2] for i in range(1, len(blocks), 2)]
    results = [
        expert_blocks(
            [b[1:] for b in group],
            [source(b[0]) for b in group],
            gates,
            gate_up_weight,
            down_weight,
        )
        for group in groups
    ]
    partial_rows = [r for result in results for r in result[3]]

    probs = {0: results[0][0], half: results[-1][0]}
    for step in range(1, half):
        probs[size - step] = results[step][0][:rows]
        probs[step] = results[step][0][rows:]
    probs = jnp.stack([probs[k] for k in range(size)]).astype(jnp.bfloat16)
    all_places = jnp.asarray([order.index(e) for e in range(size)], jnp.int32)
    probs = probs[(all_places - place) % size]
    probs = lax.all_to_all(
        probs.reshape(size * rows, local_experts), "expert", split_axis=0, concat_axis=1, tiled=True
    )
    grad_probs = jnp.sum(
        jnp.where(onehot, probs[:, None, :].astype(jnp.float32), 0.0), axis=2
    ).astype(jnp.bfloat16)

    narrow = lambda a: a.astype(jnp.bfloat16)
    to_left, to_right = partial_rows[-2], partial_rows[-1]
    for step in range(half - 1, -1, -1):
        from_right = lax.ppermute(to_left, "expert", backward).astype(jnp.float32)
        from_left = lax.ppermute(to_right, "expert", forward).astype(jnp.float32)
        if step == half - 1:
            pad = jnp.zeros((mid, width), jnp.float32)
            from_right = jnp.concatenate([from_right, pad])
            from_left = jnp.concatenate([pad, from_left])
        if step > 0:
            to_left = narrow(partial_rows[2 * step - 1].astype(jnp.float32) + from_right)
            to_right = narrow(partial_rows[2 * step].astype(jnp.float32) + from_left)
    grad_tokens = narrow(partial_rows[0].astype(jnp.float32) + from_right + from_left)

    replicas = lax.axis_size("dp")
    outer = replicas // 2
    core, row = lax.axis_index("dp") % 2, lax.axis_index("dp") // 2
    where = jnp.stack([core, row]).astype(jnp.int32)
    swap = [(i, i ^ 1) for i in range(replicas)]
    xs, gs = [b[3] for b in blocks], [b[4] for b in blocks]
    pres, hiddens = [r[1] for r in results], [r[2] for r in results]
    chunks = [(xs, pres, e) for e in range(local_experts)] + [(gs, hiddens, None)]
    shards = []
    for chunk in chunks:
        sent = weight_part(*chunk, where, replicas)
        arrived = lax.ppermute(sent, "dp", swap)
        sent, total = weight_part(*chunk, where, replicas, arrived)
        total = total.astype(jnp.float32)
        for shift in range(1, outer):
            pairs = [
                (2 * y + c, 2 * ((y + shift) % outer) + c) for y in range(outer) for c in range(2)
            ]
            total = total + lax.ppermute(sent[shift - 1], "dp", pairs).astype(jnp.float32)
        shards.append(narrow(total))
    units = down_weight.shape[1]
    weight_total = jnp.stack(
        [
            jnp.concatenate([shards[e], shards[-1][:, e * units : (e + 1) * units]], axis=1)
            for e in range(local_experts)
        ],
        axis=1,
    )
    return (grad_tokens, grad_probs, weight_total)


def solution(mesh):
    in_specs = (
        P(("dp", "expert"), None),
        P(("dp", "expert"), None),
        P(("dp", "expert"), None),
        P(("dp", "expert"), None),
        P("expert", None, None),
        P("expert", None, None),
    )
    out_specs = (P(("dp", "expert"), None), P(("dp", "expert"), None), P("dp", "expert", None))
    return jax.shard_map(
        on_device, mesh=mesh, in_specs=in_specs, out_specs=out_specs, check_vma=False
    )
```

```python
import functools

import jax
import jax.numpy as jnp
from jax import lax
from jax.experimental import pallas as pl
from jax.experimental.pallas import tpu as pltpu
from jax.sharding import PartitionSpec as P


def ring_order(size):
    half = size // 2
    return [2 * p if p < half else 2 * (size - 1 - p) + 1 for p in range(size)]


def joined(refs):
    parts = [ref[...] for ref in refs]
    return parts[0] if len(parts) == 1 else jnp.concatenate(parts, axis=0)


def expert_kernel(count, size, scalars, *refs):
    g_refs, gate_refs = refs[:count], refs[count : 2 * count]
    first, (w_in, w_out, pre_ref, hidden_ref) = 2 * count, refs[-(count + 5) : -(count + 1)]
    row_refs, total = refs[-(count + 1) : -1], refs[-1]
    e, last = pl.program_id(0), pl.num_programs(0) - 1
    units, width = w_out.shape[1:]
    x_refs = refs[first : -(count + 5)]
    pre = jnp.dot(joined(x_refs), w_in[0], preferred_element_type=jnp.float32)
    back = lax.dot_general(
        joined(g_refs), w_out[0], (((1,), (1,)), ((), ())), preferred_element_type=jnp.float32
    )
    gates = [ref[0].astype(jnp.float32) for ref in gate_refs]
    gates = gates[0] if count == 1 else jnp.concatenate(gates, axis=0)
    column = lax.broadcasted_iota(jnp.int32, gates.shape, 1) == e
    weight = jnp.sum(jnp.where(column, gates, 0.0), axis=1, keepdims=True)
    gate_pre, up_pre = pre[:, :units], pre[:, units:]
    logistic = 1.0 / (1.0 + jnp.exp(-gate_pre))
    active = gate_pre * logistic
    slope = logistic * (1.0 + gate_pre * (1.0 - logistic))
    hidden = (active * up_pre).astype(jnp.bfloat16).astype(jnp.float32)
    probs = jnp.sum(hidden * back, axis=1, keepdims=True)
    hidden_ref[0] = (weight * hidden).astype(jnp.bfloat16)
    grad_hidden = weight * back
    pre_ref[0, :, :units] = (grad_hidden * up_pre * slope).astype(jnp.bfloat16)
    pre_ref[0, :, units:] = (grad_hidden * active).astype(jnp.bfloat16)
    rows = lax.dot_general(
        pre_ref[0], w_in[0], (((1,), (1,)), ((), ())), preferred_element_type=jnp.float32
    )
    lane = lax.broadcasted_iota(jnp.int32, (rows.shape[0], total.shape[1] - width), 1)
    tail = jnp.where(lane == scalars[size] * pl.num_programs(0) + e, probs, 0.0)

    @pl.when(e == 0)
    def _():
        total[:, :width] = rows
        total[:, width:] = tail

    @pl.when(e > 0)
    def _():
        total[:, :width] += rows
        total[:, width:] += tail

    @pl.when(e == last)
    def _():
        at = 0
        for ref in row_refs:
            ref[...] = total[at : at + ref.shape[0]].astype(jnp.bfloat16)
            at += ref.shape[0]


def expert_blocks(blocks, table, gates, weight_in, weight_out):
    count = len(blocks)
    experts, width, wide = weight_in.shape
    units = weight_out.shape[1]
    sizes = [b[2] - b[1] for b in blocks]
    rows = sum(sizes)
    full = width + -(-gates.shape[0] * experts // 128) * 128
    whole = lambda n, w=width: pl.BlockSpec((n, w), lambda e, s: (0, 0))

    def gate_spec(offset, lo, n):
        return pl.BlockSpec((1, n, experts), lambda e, s: (s[offset], lo // n, 0))

    per_expert = lambda a, b: pl.BlockSpec((1, a, b), lambda e, s: (e, 0, 0))
    out = pl.pallas_call(
        functools.partial(expert_kernel, count, gates.shape[0]),
        out_shape=[
            jax.ShapeDtypeStruct((experts, rows, wide), jnp.bfloat16),
            jax.ShapeDtypeStruct((experts, rows, units), jnp.bfloat16),
        ]
        + [jax.ShapeDtypeStruct((n, full), jnp.bfloat16) for n in sizes],
        grid_spec=pltpu.PrefetchScalarGridSpec(
            num_scalar_prefetch=1,
            grid=(experts,),
            in_specs=[whole(n) for n in sizes]
            + [gate_spec(b[0], b[1], b[2] - b[1]) for b in blocks]
            + [whole(n) for n in sizes]
            + [per_expert(width, wide), per_expert(units, width)],
            out_specs=[per_expert(rows, wide), per_expert(rows, units)]
            + [whole(n, full) for n in sizes],
            scratch_shapes=[pltpu.VMEM((rows, full), jnp.float32)],
        ),
        cost_estimate=pl.CostEstimate(
            flops=2 * rows * experts * width * (2 * wide + units),
            bytes_accessed=2 * experts * width * (wide + units) + 8 * rows * width,
            transcendentals=0,
        ),
        name="experts",
    )(table, *[b[4] for b in blocks], *[gates] * count, *[b[3] for b in blocks], weight_in, weight_out)
    return out[0], out[1], out[2:]


def weight_kernel(x_rows, p_rows, start, depth, *refs):
    x_refs, p_refs = refs[: len(x_rows)], refs[len(x_rows) : len(x_rows) + len(p_rows)]
    sent, kept, held, gradients, result, x_sems, p_sems, sems = refs[len(x_rows) + len(p_rows) :]
    outer, experts = sent.shape[0], p_refs[0].shape[0]
    size = sent.shape[2] // experts

    core, mine = lax.axis_index("dp") & 1, lax.axis_index("dp") >> 1

    def slabs(i):
        for place in range(outer):
            block = 2 * lax.rem(mine + 1 + place, outer) + (1 - core if i == 0 else core)
            column = pl.multiple_of(block * depth, depth)
            row = 0
            for k, n in enumerate(x_rows):
                yield pltpu.make_async_copy(
                    x_refs[k].at[:, pl.ds(column, depth)],
                    held.at[i, row : row + n, place * depth : (place + 1) * depth],
                    x_sems.at[i, place, k],
                )
                row += n

    def gradient_copies():
        row = 0
        for k, n in enumerate(p_rows):
            for e in range(experts):
                yield pltpu.make_async_copy(
                    p_refs[k].at[e, :, start : start + size],
                    gradients.at[row : row + n, e * size : (e + 1) * size],
                    p_sems.at[k, e],
                )
            row += n

    for copy in [*slabs(0), *gradient_copies(), *slabs(1)]:
        copy.start()
    for copy in gradient_copies():
        copy.wait()
    stores = []
    for i, out in enumerate((sent, kept)):
        for copy in slabs(i):
            copy.wait()
        part = lax.dot_general(
            held[i], gradients[...], (((0,), (0,)), ((), ())), preferred_element_type=jnp.float32
        )
        result[i] = part.astype(jnp.bfloat16).reshape(result.shape[1:])
        stores.append(pltpu.make_async_copy(result.at[i], out, sems.at[i]))
        stores[-1].start()
    for store in stores:
        store.wait()


def weight_parts(xs, ps, start, size, replicas):
    width = xs[0].shape[1]
    experts = ps[0].shape[0]
    outer, depth = replicas // 2, width // replicas
    x_rows, p_rows = [x.shape[0] for x in xs], [p.shape[1] for p in ps]
    rows, columns = sum(x_rows), experts * size

    anywhere = pl.BlockSpec(memory_space=pl.ANY)
    return pl.pallas_call(
        functools.partial(weight_kernel, x_rows, p_rows, start, depth),
        out_shape=[jax.ShapeDtypeStruct((outer, depth, columns), jnp.bfloat16)] * 2,
        in_specs=[anywhere] * (len(xs) + len(ps)),
        out_specs=[anywhere] * 2,
        scratch_shapes=[
            pltpu.VMEM((2, rows, outer * depth), jnp.bfloat16),
            pltpu.VMEM((rows, columns), jnp.bfloat16),
            pltpu.VMEM((2, outer, depth, columns), jnp.bfloat16),
            pltpu.SemaphoreType.DMA((2, outer, len(xs))),
            pltpu.SemaphoreType.DMA((len(ps), experts)),
            pltpu.SemaphoreType.DMA((2,)),
        ],
        cost_estimate=pl.CostEstimate(
            flops=2 * rows * width * columns,
            bytes_accessed=2 * (rows * (width + columns) + width * columns),
            transcendentals=0,
        ),
        name="weights",
    )(*xs, *ps)


def place_kernel(count, *refs):
    total = refs[0][...].astype(jnp.float32)
    for ref in refs[1:count]:
        total += ref[...].astype(jnp.float32)
    out = refs[-1]
    size = out.shape[2]
    for e in range(out.shape[1]):
        out[:, e, :] = total[:, e * size : (e + 1) * size].astype(jnp.bfloat16)


def place_chunk(pieces, at, experts, columns, held=None):
    depth, size = pieces[0].shape[1], pieces[0].shape[2] // experts
    tile = depth
    specs = [
        pl.BlockSpec((None, tile, experts * size), lambda i, last=p.shape[0] - 1: (last, i, 0))
        for p in pieces
    ]
    args = list(pieces) + ([] if held is None else [held])
    return pl.pallas_call(
        functools.partial(place_kernel, len(pieces)),
        out_shape=jax.ShapeDtypeStruct((depth, experts, columns), jnp.bfloat16),
        grid=(depth // tile,),
        in_specs=specs
        + ([] if held is None else [pl.BlockSpec(memory_space=pl.ANY)]),
        out_specs=pl.BlockSpec((tile, experts, size), lambda i: (i, 0, at)),
        input_output_aliases={} if held is None else {len(pieces): 0},
        name="place",
    )(*args)


def layer(tokens, out_grad, expert_ids, gate_probs, gate_up_weight, down_weight):
    rows, width = tokens.shape
    local_experts = gate_up_weight.shape[0]
    size = lax.axis_size("expert")
    expert_count = local_experts * size
    half, mid = size // 2, rows // 2
    order = ring_order(size)
    forward = [(order[p], order[(p + 1) % size]) for p in range(size)]
    backward = [(b, a) for a, b in forward]
    me = lax.axis_index("expert")
    experts = jnp.arange(expert_count, dtype=jnp.int32)
    onehot = expert_ids[:, :, None] == experts[None, None, :]
    dense_gates = jnp.sum(
        jnp.where(onehot, gate_probs[:, :, None].astype(jnp.float32), 0.0), axis=1
    ).astype(jnp.bfloat16)
    gates = lax.all_to_all(dense_gates, "expert", split_axis=1, concat_axis=0, tiled=True)
    gates = gates.reshape(size, rows, local_experts)
    followers = [[order[(order.index(e) + k) % size] for k in range(size)] for e in range(size)]
    mine = lax.broadcasted_iota(jnp.int32, (size, size), 0) == me
    table = jnp.sum(jnp.where(mine, jnp.asarray(followers, jnp.int32), 0), axis=0)
    table = jnp.concatenate([table, me[None].astype(jnp.int32)])

    blocks = [(0, 0, rows, tokens, out_grad)]
    left, right = (tokens, out_grad), (tokens, out_grad)
    for step in range(1, half + 1):
        if step == half:
            left, right = tuple(a[:mid] for a in left), tuple(a[mid:] for a in right)
        xl = lax.ppermute(left[0], "expert", forward)
        xr = lax.ppermute(right[0], "expert", backward)
        left = (xl, lax.ppermute(left[1], "expert", forward))
        right = (xr, lax.ppermute(right[1], "expert", backward))
        if step < half:
            blocks.append((size - step, 0, rows) + left)
            blocks.append((step, 0, rows) + right)
    blocks.append((half, 0, mid) + left)
    blocks.append((half, mid, rows) + right)

    groups = [blocks[:3]] + [blocks[i : i + 2] for i in range(3, len(blocks), 2)]
    results = []
    for group in groups:
        results.append(
            expert_blocks(group, table, gates, gate_up_weight, down_weight)
        )
    partial_rows = [r for result in results for r in result[2]]

    narrow = lambda a: a.astype(jnp.bfloat16)
    to_left, to_right = partial_rows[-2], partial_rows[-1]
    for step in range(half - 1, -1, -1):
        from_right = lax.ppermute(to_left, "expert", backward).astype(jnp.float32)
        from_left = lax.ppermute(to_right, "expert", forward).astype(jnp.float32)
        if step == half - 1:
            pad = jnp.zeros((mid, from_left.shape[1]), jnp.float32)
            from_right = jnp.concatenate([from_right, pad])
            from_left = jnp.concatenate([pad, from_left])
        if step > 0:
            to_left = narrow(partial_rows[2 * step - 1].astype(jnp.float32) + from_right)
            to_right = narrow(partial_rows[2 * step].astype(jnp.float32) + from_left)
    returned = narrow(partial_rows[0].astype(jnp.float32) + from_right + from_left)
    grad_tokens = returned[:, :width]
    probs = returned[:, width : width + expert_count].astype(jnp.float32)
    grad_probs = narrow(jnp.sum(jnp.where(onehot, probs[:, None, :], 0.0), axis=2))

    replicas = lax.axis_size("dp")
    outer = replicas // 2
    swap = [(i, i ^ 1) for i in range(replicas)]
    xs, gs = [b[3] for b in blocks], [b[4] for b in blocks]
    pres, hiddens = [r[0] for r in results], [r[1] for r in results]
    units = down_weight.shape[1]
    third = 2 * units // 3
    chunks = [(xs, pres, 2 * third, third), (gs, hiddens, 0, units), (xs, pres, 0, 2 * third)]
    places = [2, 2, 0]
    parts = []
    for chunk in chunks:
        parts += weight_parts(*chunk, replicas)
    weight_total = None
    for number, at in enumerate(places):
        sent, kept = parts[2 * number : 2 * number + 2]
        arrived = lax.ppermute(sent, "dp", swap)
        pieces = [kept, arrived]
        for shift in range(1, outer):
            pairs = [
                (2 * y + c, 2 * ((y + shift) % outer) + c) for y in range(outer) for c in range(2)
            ]
            both = kept[shift - 1].astype(jnp.float32) + arrived[shift - 1].astype(jnp.float32)
            pieces.append(lax.ppermute(narrow(both)[None], "dp", pairs))
        weight_total = place_chunk(pieces, at, local_experts, 3 * units, weight_total)
    return (grad_tokens, grad_probs, weight_total)


def solution(mesh):
    in_specs = (
        P(("dp", "expert"), None),
        P(("dp", "expert"), None),
        P(("dp", "expert"), None),
        P(("dp", "expert"), None),
        P("expert", None, None),
        P("expert", None, None),
    )
    out_specs = (P(("dp", "expert"), None), P(("dp", "expert"), None), P("dp", "expert", None))
    return jax.shard_map(layer, mesh=mesh, in_specs=in_specs, out_specs=out_specs, check_vma=False)
```

```python
import functools

import jax
import jax.numpy as jnp
from jax import lax
from jax.experimental import pallas as pl
from jax.experimental.pallas import tpu as pltpu
from jax.sharding import PartitionSpec as P


def ring_order(size):
    half = size // 2
    return [2 * p if p < half else 2 * (size - 1 - p) + 1 for p in range(size)]


def joined(refs):
    parts = [ref[...] for ref in refs]
    return parts[0] if len(parts) == 1 else jnp.concatenate(parts, axis=0)


def row_totals(total, rows, tail, row_refs):
    e, last = pl.program_id(0), pl.num_programs(0) - 1
    width = rows.shape[1]

    @pl.when(e == 0)
    def _():
        total[:, :width] = rows
        total[:, width:] = tail

    @pl.when(e > 0)
    def _():
        total[:, :width] += rows
        total[:, width:] += tail

    @pl.when(e == last)
    def _():
        at = 0
        for ref in row_refs:
            ref[...] = total[at : at + ref.shape[0]].astype(jnp.bfloat16)
            at += ref.shape[0]


def times_transposed(left, right):
    return lax.dot_general(left, right, (((1,), (1,)), ((), ())), preferred_element_type=jnp.float32)


def expert_kernel(count, size, with_rows, scalars, *refs):
    x_refs, g_refs, gate_refs = refs[:count], refs[count : 2 * count], refs[2 * count : 3 * count]
    w_in, w_out, pre_ref, hidden_ref = refs[3 * count : 3 * count + 4]
    outs = refs[3 * count + 4 :]
    e = pl.program_id(0)
    units = w_out.shape[1]
    pre = jnp.dot(joined(x_refs), w_in[0], preferred_element_type=jnp.float32)
    back = times_transposed(joined(g_refs), w_out[0])
    gates = [ref[0].astype(jnp.float32) for ref in gate_refs]
    gates = gates[0] if count == 1 else jnp.concatenate(gates, axis=0)
    column = lax.broadcasted_iota(jnp.int32, gates.shape, 1) == e
    weight = jnp.sum(jnp.where(column, gates, 0.0), axis=1, keepdims=True)
    gate_pre, up_pre = pre[:, :units], pre[:, units:]
    logistic = 1.0 / (1.0 + jnp.exp(-gate_pre))
    active = gate_pre * logistic
    slope = logistic * (1.0 + gate_pre * (1.0 - logistic))
    hidden = (active * up_pre).astype(jnp.bfloat16).astype(jnp.float32)
    probs = jnp.sum(hidden * back, axis=1, keepdims=True)
    hidden_ref[0] = (weight * hidden).astype(jnp.bfloat16)
    grad_hidden = weight * back
    pre_ref[0, :, :units] = (grad_hidden * up_pre * slope).astype(jnp.bfloat16)
    pre_ref[0, :, units:] = (grad_hidden * active).astype(jnp.bfloat16)
    extra = outs[-1].shape[-1] - (w_out.shape[2] if with_rows else 0)
    lane = lax.broadcasted_iota(jnp.int32, (pre.shape[0], extra), 1)
    tail = jnp.where(lane == scalars[size] * pl.num_programs(0) + e, probs, 0.0)
    if with_rows:
        row_totals(outs[-1], times_transposed(pre_ref[0], w_in[0]), tail, outs[:-1])
    else:
        outs[0][0] = tail


def row_kernel(count, *refs):
    p_refs, tail_refs, w_in = refs[:count], refs[count : 2 * count], refs[2 * count]
    parts = [ref[0] for ref in p_refs]
    tails = [ref[0] for ref in tail_refs]
    rows = times_transposed(jnp.concatenate(parts, axis=0), w_in[0])
    row_totals(refs[-1], rows, jnp.concatenate(tails, axis=0), refs[2 * count + 1 : -1])


def row_blocks(pres, tails, sizes, weight_in):
    experts, width, wide = weight_in.shape
    rows, full = sum(sizes), width + tails[0].shape[2]
    per_expert = lambda a: pl.BlockSpec((1,) + a.shape[1:], lambda e: (e, 0, 0))
    return pl.pallas_call(
        functools.partial(row_kernel, len(pres)),
        out_shape=[jax.ShapeDtypeStruct((n, full), jnp.bfloat16) for n in sizes],
        grid=(experts,),
        in_specs=[per_expert(a) for a in [*pres, *tails, weight_in]],
        out_specs=[pl.BlockSpec((n, full), lambda e: (0, 0)) for n in sizes],
        scratch_shapes=[pltpu.VMEM((rows, full), jnp.float32)],
        cost_estimate=pl.CostEstimate(
            flops=2 * rows * experts * width * wide,
            bytes_accessed=2 * experts * width * wide + 4 * rows * width,
            transcendentals=0,
        ),
        name="rows",
    )(*pres, *tails, weight_in)


def expert_blocks(blocks, table, gates, weight_in, weight_out, with_rows):
    count = len(blocks)
    experts, width, wide = weight_in.shape
    units = weight_out.shape[1]
    sizes = [b[2] - b[1] for b in blocks]
    rows = sum(sizes)
    extra = -(-gates.shape[0] * experts // 128) * 128
    whole = lambda n, w=width: pl.BlockSpec((n, w), lambda e, s: (0, 0))

    def gate_spec(offset, lo, n):
        return pl.BlockSpec((1, n, experts), lambda e, s: (s[offset], lo // n, 0))

    per_expert = lambda a, b: pl.BlockSpec((1, a, b), lambda e, s: (e, 0, 0))
    if with_rows:
        more = [jax.ShapeDtypeStruct((n, width + extra), jnp.bfloat16) for n in sizes]
        more_specs = [whole(n, width + extra) for n in sizes]
        scratch = [pltpu.VMEM((rows, width + extra), jnp.float32)]
    else:
        more = [jax.ShapeDtypeStruct((experts, rows, extra), jnp.float32)]
        more_specs, scratch = [per_expert(rows, extra)], []
    out = pl.pallas_call(
        functools.partial(expert_kernel, count, gates.shape[0], with_rows),
        out_shape=[
            jax.ShapeDtypeStruct((experts, rows, wide), jnp.bfloat16),
            jax.ShapeDtypeStruct((experts, rows, units), jnp.bfloat16),
        ]
        + more,
        grid_spec=pltpu.PrefetchScalarGridSpec(
            num_scalar_prefetch=1,
            grid=(experts,),
            in_specs=[whole(n) for n in sizes] * 2
            + [gate_spec(b[0], b[1], b[2] - b[1]) for b in blocks]
            + [per_expert(width, wide), per_expert(units, width)],
            out_specs=[per_expert(rows, wide), per_expert(rows, units)] + more_specs,
            scratch_shapes=scratch,
        ),
        cost_estimate=pl.CostEstimate(
            flops=2 * rows * experts * width * ((1 + with_rows) * wide + units),
            bytes_accessed=2 * experts * width * (wide + units) + 8 * rows * width,
            transcendentals=0,
        ),
        name="experts",
    )(
        table,
        *[b[3] for b in blocks],
        *[b[4] for b in blocks],
        *[gates] * count,
        weight_in,
        weight_out,
    )
    return out[0], out[1], out[2:]


def weight_kernel(x_rows, p_rows, start, depth, *refs):
    x_refs, p_refs = refs[: len(x_rows)], refs[len(x_rows) : len(x_rows) + len(p_rows)]
    sent, kept, held, gradients, result, x_sems, p_sems, sems = refs[len(x_rows) + len(p_rows) :]
    outer, experts = sent.shape[0], p_refs[0].shape[0]
    size = sent.shape[2] // experts

    core, mine = lax.axis_index("dp") & 1, lax.axis_index("dp") >> 1

    def slabs(i):
        for place in range(outer):
            block = 2 * lax.rem(mine + 1 + place, outer) + (1 - core if i == 0 else core)
            column = pl.multiple_of(block * depth, depth)
            row = 0
            for k, n in enumerate(x_rows):
                yield pltpu.make_async_copy(
                    x_refs[k].at[:, pl.ds(column, depth)],
                    held.at[i, row : row + n, place * depth : (place + 1) * depth],
                    x_sems.at[i, place, k],
                )
                row += n

    def gradient_copies():
        row = 0
        for k, n in enumerate(p_rows):
            for e in range(experts):
                yield pltpu.make_async_copy(
                    p_refs[k].at[e, :, start : start + size],
                    gradients.at[row : row + n, e * size : (e + 1) * size],
                    p_sems.at[k, e],
                )
            row += n

    for copy in [*slabs(0), *gradient_copies(), *slabs(1)]:
        copy.start()
    for copy in gradient_copies():
        copy.wait()
    stores = []
    for i, out in enumerate((sent, kept)):
        for copy in slabs(i):
            copy.wait()
        part = lax.dot_general(
            held[i], gradients[...], (((0,), (0,)), ((), ())), preferred_element_type=jnp.float32
        )
        result[i] = part.astype(jnp.bfloat16).reshape(result.shape[1:])
        stores.append(pltpu.make_async_copy(result.at[i], out, sems.at[i]))
        stores[-1].start()
    for store in stores:
        store.wait()


def weight_parts(xs, ps, start, size, replicas):
    width = xs[0].shape[1]
    experts = ps[0].shape[0]
    outer, depth = replicas // 2, width // replicas
    x_rows, p_rows = [x.shape[0] for x in xs], [p.shape[1] for p in ps]
    rows, columns = sum(x_rows), experts * size

    anywhere = pl.BlockSpec(memory_space=pl.ANY)
    return pl.pallas_call(
        functools.partial(weight_kernel, x_rows, p_rows, start, depth),
        out_shape=[jax.ShapeDtypeStruct((outer, depth, columns), jnp.bfloat16)] * 2,
        in_specs=[anywhere] * (len(xs) + len(ps)),
        out_specs=[anywhere] * 2,
        scratch_shapes=[
            pltpu.VMEM((2, rows, outer * depth), jnp.bfloat16),
            pltpu.VMEM((rows, columns), jnp.bfloat16),
            pltpu.VMEM((2, outer, depth, columns), jnp.bfloat16),
            pltpu.SemaphoreType.DMA((2, outer, len(xs))),
            pltpu.SemaphoreType.DMA((len(ps), experts)),
            pltpu.SemaphoreType.DMA((2,)),
        ],
        cost_estimate=pl.CostEstimate(
            flops=2 * rows * width * columns,
            bytes_accessed=2 * (rows * (width + columns) + width * columns),
            transcendentals=0,
        ),
        name="weights",
    )(*xs, *ps)


def place_kernel(count, *refs):
    total = refs[0][...].astype(jnp.float32)
    for ref in refs[1:count]:
        total += ref[...].astype(jnp.float32)
    out = refs[-1]
    size = out.shape[2]
    for e in range(out.shape[1]):
        out[:, e, :] = total[:, e * size : (e + 1) * size].astype(jnp.bfloat16)


def place_chunk(pieces, at, experts, columns, held=None):
    depth, size = pieces[0].shape[1], pieces[0].shape[2] // experts
    tile = depth
    specs = [
        pl.BlockSpec((None, tile, experts * size), lambda i, last=p.shape[0] - 1: (last, i, 0))
        for p in pieces
    ]
    args = list(pieces) + ([] if held is None else [held])
    return pl.pallas_call(
        functools.partial(place_kernel, len(pieces)),
        out_shape=jax.ShapeDtypeStruct((depth, experts, columns), jnp.bfloat16),
        grid=(depth // tile,),
        in_specs=specs
        + ([] if held is None else [pl.BlockSpec(memory_space=pl.ANY)]),
        out_specs=pl.BlockSpec((tile, experts, size), lambda i: (i, 0, at)),
        input_output_aliases={} if held is None else {len(pieces): 0},
        name="place",
    )(*args)


def layer(tokens, out_grad, expert_ids, gate_probs, gate_up_weight, down_weight):
    rows, width = tokens.shape
    local_experts = gate_up_weight.shape[0]
    size = lax.axis_size("expert")
    expert_count = local_experts * size
    half, mid = size // 2, rows // 2
    order = ring_order(size)
    forward = [(order[p], order[(p + 1) % size]) for p in range(size)]
    backward = [(b, a) for a, b in forward]
    me = lax.axis_index("expert")
    experts = jnp.arange(expert_count, dtype=jnp.int32)
    onehot = expert_ids[:, :, None] == experts[None, None, :]
    dense_gates = jnp.sum(
        jnp.where(onehot, gate_probs[:, :, None].astype(jnp.float32), 0.0), axis=1
    ).astype(jnp.bfloat16)
    gates = lax.all_to_all(dense_gates, "expert", split_axis=1, concat_axis=0, tiled=True)
    gates = gates.reshape(size, rows, local_experts)
    followers = [[order[(order.index(e) + k) % size] for k in range(size)] for e in range(size)]
    mine = lax.broadcasted_iota(jnp.int32, (size, size), 0) == me
    table = jnp.sum(jnp.where(mine, jnp.asarray(followers, jnp.int32), 0), axis=0)
    table = jnp.concatenate([table, me[None].astype(jnp.int32)])

    blocks = [(0, 0, rows, tokens, out_grad)]
    left, right = (tokens, out_grad), (tokens, out_grad)
    for step in range(1, half + 1):
        if step == half:
            left, right = tuple(a[:mid] for a in left), tuple(a[mid:] for a in right)
        xl = lax.ppermute(left[0], "expert", forward)
        xr = lax.ppermute(right[0], "expert", backward)
        left = (xl, lax.ppermute(left[1], "expert", forward))
        right = (xr, lax.ppermute(right[1], "expert", backward))
        if step < half:
            blocks.append((size - step, 0, rows) + left)
            blocks.append((step, 0, rows) + right)
    blocks.append((half, 0, mid) + left)
    blocks.append((half, mid, rows) + right)

    groups = [blocks[:3]] + [blocks[i : i + 2] for i in range(3, len(blocks), 2)]
    results = []
    for number, group in enumerate(groups):
        results.append(
            expert_blocks(group, table, gates, gate_up_weight, down_weight, number < half - 2)
        )
    partial_rows = [r for result in results[:-2] for r in result[2]]
    partial_rows += row_blocks(
        [r[0] for r in results[-2:]],
        [r[2][0] for r in results[-2:]],
        [rows, rows, mid, mid],
        gate_up_weight,
    )

    narrow = lambda a: a.astype(jnp.bfloat16)
    to_left, to_right = partial_rows[-2], partial_rows[-1]
    for step in range(half - 1, -1, -1):
        from_right = lax.ppermute(to_left, "expert", backward).astype(jnp.float32)
        from_left = lax.ppermute(to_right, "expert", forward).astype(jnp.float32)
        if step == half - 1:
            pad = jnp.zeros((mid, from_left.shape[1]), jnp.float32)
            from_right = jnp.concatenate([from_right, pad])
            from_left = jnp.concatenate([pad, from_left])
        if step > 0:
            to_left = narrow(partial_rows[2 * step - 1].astype(jnp.float32) + from_right)
            to_right = narrow(partial_rows[2 * step].astype(jnp.float32) + from_left)
    returned = narrow(partial_rows[0].astype(jnp.float32) + from_right + from_left)
    grad_tokens = returned[:, :width]
    probs = returned[:, width : width + expert_count].astype(jnp.float32)
    grad_probs = narrow(jnp.sum(jnp.where(onehot, probs[:, None, :], 0.0), axis=2))

    replicas = lax.axis_size("dp")
    outer = replicas // 2
    swap = [(i, i ^ 1) for i in range(replicas)]
    xs, gs = [b[3] for b in blocks], [b[4] for b in blocks]
    pres, hiddens = [r[0] for r in results], [r[1] for r in results]
    units = down_weight.shape[1]
    third = 2 * units // 3
    chunks = [(xs, pres, 2 * third, third), (gs, hiddens, 0, units), (xs, pres, 0, 2 * third)]
    places = [2, 2, 0]
    parts = []
    for chunk in chunks:
        parts += weight_parts(*chunk, replicas)
    weight_total = None
    for number, at in enumerate(places):
        sent, kept = parts[2 * number : 2 * number + 2]
        arrived = lax.ppermute(sent, "dp", swap)
        pieces = [kept, arrived]
        for shift in range(1, outer):
            pairs = [
                (2 * y + c, 2 * ((y + shift) % outer) + c) for y in range(outer) for c in range(2)
            ]
            both = kept[shift - 1].astype(jnp.float32) + arrived[shift - 1].astype(jnp.float32)
            pieces.append(lax.ppermute(narrow(both)[None], "dp", pairs))
        weight_total = place_chunk(pieces, at, local_experts, 3 * units, weight_total)
    return (grad_tokens, grad_probs, weight_total)


def solution(mesh):
    in_specs = (
        P(("dp", "expert"), None),
        P(("dp", "expert"), None),
        P(("dp", "expert"), None),
        P(("dp", "expert"), None),
        P("expert", None, None),
        P("expert", None, None),
    )
    out_specs = (P(("dp", "expert"), None), P(("dp", "expert"), None), P("dp", "expert", None))
    return jax.shard_map(layer, mesh=mesh, in_specs=in_specs, out_specs=out_specs, check_vma=False)
```

```python
import functools

import jax
import jax.numpy as jnp
from jax import lax
from jax.experimental import pallas as pl
from jax.experimental.pallas import tpu as pltpu
from jax.sharding import PartitionSpec as P


def ring_order(size):
    half = size // 2
    return [2 * p if p < half else 2 * (size - 1 - p) + 1 for p in range(size)]


def joined(refs):
    parts = [ref[...] for ref in refs]
    return parts[0] if len(parts) == 1 else jnp.concatenate(parts, axis=0)


def row_totals(total, rows, tail, row_refs):
    e, last = pl.program_id(0), pl.num_programs(0) - 1
    width = rows.shape[1]

    @pl.when(e == 0)
    def _():
        total[:, :width] = rows
        total[:, width:] = tail

    @pl.when(e > 0)
    def _():
        total[:, :width] += rows
        total[:, width:] += tail

    @pl.when(e == last)
    def _():
        at = 0
        for left, right in zip(row_refs[::2], row_refs[1::2]):
            span, split = slice(at, at + left.shape[0]), left.shape[1]
            left[...] = total[span, :split].astype(jnp.bfloat16)
            right[...] = total[span, split:].astype(jnp.bfloat16)
            at += left.shape[0]


def times_transposed(left, right):
    return lax.dot_general(left, right, (((1,), (1,)), ((), ())), preferred_element_type=jnp.float32)


def expert_kernel(count, size, with_rows, scalars, *refs):
    x_refs, g_refs, gate_refs = refs[:count], refs[count : 2 * count], refs[2 * count : 3 * count]
    w_in, w_out, pre_ref, hidden_ref = refs[3 * count : 3 * count + 4]
    outs = refs[3 * count + 4 :]
    e = pl.program_id(0)
    units = w_out.shape[1]
    pre = jnp.dot(joined(x_refs), w_in[0], preferred_element_type=jnp.float32)
    back = times_transposed(joined(g_refs), w_out[0])
    gates = [ref[0].astype(jnp.float32) for ref in gate_refs]
    gates = gates[0] if count == 1 else jnp.concatenate(gates, axis=0)
    column = lax.broadcasted_iota(jnp.int32, gates.shape, 1) == e
    weight = jnp.sum(jnp.where(column, gates, 0.0), axis=1, keepdims=True)
    gate_pre, up_pre = pre[:, :units], pre[:, units:]
    logistic = 1.0 / (1.0 + jnp.exp(-gate_pre))
    active = gate_pre * logistic
    slope = logistic * (1.0 + gate_pre * (1.0 - logistic))
    hidden = (active * up_pre).astype(jnp.bfloat16).astype(jnp.float32)
    probs = jnp.sum(hidden * back, axis=1, keepdims=True)
    hidden_ref[0] = (weight * hidden).astype(jnp.bfloat16)
    grad_hidden = weight * back
    pre_ref[0, :, :units] = (grad_hidden * up_pre * slope).astype(jnp.bfloat16)
    pre_ref[0, :, units:] = (grad_hidden * active).astype(jnp.bfloat16)
    extra = outs[-1].shape[-1] - (w_out.shape[2] if with_rows else 0)
    lane = lax.broadcasted_iota(jnp.int32, (pre.shape[0], extra), 1)
    tail = jnp.where(lane == scalars[size] * pl.num_programs(0) + e, probs, 0.0)
    if with_rows:
        row_totals(outs[-1], times_transposed(pre_ref[0], w_in[0]), tail, outs[:-1])
    else:
        outs[0][0] = tail


def row_kernel(count, *refs):
    p_refs, tail_refs, w_in = refs[:count], refs[count : 2 * count], refs[2 * count]
    parts = [ref[0] for ref in p_refs]
    tails = [ref[0] for ref in tail_refs]
    rows = times_transposed(jnp.concatenate(parts, axis=0), w_in[0])
    row_totals(refs[-1], rows, jnp.concatenate(tails, axis=0), refs[2 * count + 1 : -1])


def row_blocks(pres, tails, sizes, weight_in):
    experts, width, wide = weight_in.shape
    rows, full = sum(sizes), width + tails[0].shape[2]
    halves = (width // 2, full - width // 2)
    per_expert = lambda a: pl.BlockSpec((1,) + a.shape[1:], lambda e: (e, 0, 0))
    return pl.pallas_call(
        functools.partial(row_kernel, len(pres)),
        out_shape=[jax.ShapeDtypeStruct((n, w), jnp.bfloat16) for n in sizes for w in halves],
        grid=(experts,),
        in_specs=[per_expert(a) for a in [*pres, *tails, weight_in]],
        out_specs=[pl.BlockSpec((n, w), lambda e: (0, 0)) for n in sizes for w in halves],
        scratch_shapes=[pltpu.VMEM((rows, full), jnp.float32)],
        cost_estimate=pl.CostEstimate(
            flops=2 * rows * experts * width * wide,
            bytes_accessed=2 * experts * width * wide + 4 * rows * width,
            transcendentals=0,
        ),
        name="rows",
    )(*pres, *tails, weight_in)


def expert_blocks(blocks, table, gates, weight_in, weight_out, with_rows):
    count = len(blocks)
    experts, width, wide = weight_in.shape
    units = weight_out.shape[1]
    sizes = [b[2] - b[1] for b in blocks]
    rows = sum(sizes)
    extra = -(-gates.shape[0] * experts // 128) * 128
    whole = lambda n, w=width: pl.BlockSpec((n, w), lambda e, s: (0, 0))

    def gate_spec(offset, lo, n):
        return pl.BlockSpec((1, n, experts), lambda e, s: (s[offset], lo // n, 0))

    per_expert = lambda a, b: pl.BlockSpec((1, a, b), lambda e, s: (e, 0, 0))
    if with_rows:
        pieces = [(n, w) for n in sizes for w in (width // 2, width - width // 2 + extra)]
        more = [jax.ShapeDtypeStruct(p, jnp.bfloat16) for p in pieces]
        more_specs = [whole(*p) for p in pieces]
        scratch = [pltpu.VMEM((rows, width + extra), jnp.float32)]
    else:
        more = [jax.ShapeDtypeStruct((experts, rows, extra), jnp.float32)]
        more_specs, scratch = [per_expert(rows, extra)], []
    out = pl.pallas_call(
        functools.partial(expert_kernel, count, gates.shape[0], with_rows),
        out_shape=[
            jax.ShapeDtypeStruct((experts, rows, wide), jnp.bfloat16),
            jax.ShapeDtypeStruct((experts, rows, units), jnp.bfloat16),
        ]
        + more,
        grid_spec=pltpu.PrefetchScalarGridSpec(
            num_scalar_prefetch=1,
            grid=(experts,),
            in_specs=[whole(n) for n in sizes] * 2
            + [gate_spec(b[0], b[1], b[2] - b[1]) for b in blocks]
            + [per_expert(width, wide), per_expert(units, width)],
            out_specs=[per_expert(rows, wide), per_expert(rows, units)] + more_specs,
            scratch_shapes=scratch,
        ),
        cost_estimate=pl.CostEstimate(
            flops=2 * rows * experts * width * ((1 + with_rows) * wide + units),
            bytes_accessed=2 * experts * width * (wide + units) + 8 * rows * width,
            transcendentals=0,
        ),
        name="experts",
    )(
        table,
        *[b[3] for b in blocks],
        *[b[4] for b in blocks],
        *[gates] * count,
        weight_in,
        weight_out,
    )
    return out[0], out[1], out[2:]


def weight_kernel(x_rows, p_rows, start, depth, *refs):
    x_refs, p_refs = refs[: len(x_rows)], refs[len(x_rows) : len(x_rows) + len(p_rows)]
    sent, kept, held, gradients, result, x_sems, p_sems, sems = refs[len(x_rows) + len(p_rows) :]
    outer, experts = sent.shape[0], p_refs[0].shape[0]
    size = sent.shape[2] // experts

    core, mine = lax.axis_index("dp") & 1, lax.axis_index("dp") >> 1

    def slabs(i):
        for place in range(outer):
            block = 2 * lax.rem(mine + 1 + place, outer) + (1 - core if i == 0 else core)
            column = pl.multiple_of(block * depth, depth)
            row = 0
            for k, n in enumerate(x_rows):
                yield pltpu.make_async_copy(
                    x_refs[k].at[:, pl.ds(column, depth)],
                    held.at[i, row : row + n, place * depth : (place + 1) * depth],
                    x_sems.at[i, place, k],
                )
                row += n

    def gradient_copies():
        row = 0
        for k, n in enumerate(p_rows):
            for e in range(experts):
                yield pltpu.make_async_copy(
                    p_refs[k].at[e, :, start : start + size],
                    gradients.at[row : row + n, e * size : (e + 1) * size],
                    p_sems.at[k, e],
                )
            row += n

    for copy in [*slabs(0), *gradient_copies(), *slabs(1)]:
        copy.start()
    for copy in gradient_copies():
        copy.wait()
    stores = []
    for i, out in enumerate((sent, kept)):
        for copy in slabs(i):
            copy.wait()
        part = lax.dot_general(
            held[i], gradients[...], (((0,), (0,)), ((), ())), preferred_element_type=jnp.float32
        )
        result[i] = part.astype(jnp.bfloat16).reshape(result.shape[1:])
        stores.append(pltpu.make_async_copy(result.at[i], out, sems.at[i]))
        stores[-1].start()
    for store in stores:
        store.wait()


def weight_parts(xs, ps, start, size, replicas):
    width = xs[0].shape[1]
    experts = ps[0].shape[0]
    outer, depth = replicas // 2, width // replicas
    x_rows, p_rows = [x.shape[0] for x in xs], [p.shape[1] for p in ps]
    rows, columns = sum(x_rows), experts * size

    anywhere = pl.BlockSpec(memory_space=pl.ANY)
    return pl.pallas_call(
        functools.partial(weight_kernel, x_rows, p_rows, start, depth),
        out_shape=[jax.ShapeDtypeStruct((outer, depth, columns), jnp.bfloat16)] * 2,
        in_specs=[anywhere] * (len(xs) + len(ps)),
        out_specs=[anywhere] * 2,
        scratch_shapes=[
            pltpu.VMEM((2, rows, outer * depth), jnp.bfloat16),
            pltpu.VMEM((rows, columns), jnp.bfloat16),
            pltpu.VMEM((2, outer, depth, columns), jnp.bfloat16),
            pltpu.SemaphoreType.DMA((2, outer, len(xs))),
            pltpu.SemaphoreType.DMA((len(ps), experts)),
            pltpu.SemaphoreType.DMA((2,)),
        ],
        cost_estimate=pl.CostEstimate(
            flops=2 * rows * width * columns,
            bytes_accessed=2 * (rows * (width + columns) + width * columns),
            transcendentals=0,
        ),
        name="weights",
    )(*xs, *ps)


def place_kernel(count, *refs):
    total = refs[0][...].astype(jnp.float32)
    for ref in refs[1:count]:
        total += ref[...].astype(jnp.float32)
    out = refs[-1]
    size = out.shape[2]
    for e in range(out.shape[1]):
        out[:, e, :] = total[:, e * size : (e + 1) * size].astype(jnp.bfloat16)


def place_chunk(pieces, at, experts, columns, held=None):
    depth, size = pieces[0].shape[1], pieces[0].shape[2] // experts
    tile = depth
    specs = [
        pl.BlockSpec((None, tile, experts * size), lambda i, last=p.shape[0] - 1: (last, i, 0))
        for p in pieces
    ]
    args = list(pieces) + ([] if held is None else [held])
    return pl.pallas_call(
        functools.partial(place_kernel, len(pieces)),
        out_shape=jax.ShapeDtypeStruct((depth, experts, columns), jnp.bfloat16),
        grid=(depth // tile,),
        in_specs=specs
        + ([] if held is None else [pl.BlockSpec(memory_space=pl.ANY)]),
        out_specs=pl.BlockSpec((tile, experts, size), lambda i: (i, 0, at)),
        input_output_aliases={} if held is None else {len(pieces): 0},
        name="place",
    )(*args)


def layer(tokens, out_grad, expert_ids, gate_probs, gate_up_weight, down_weight):
    rows, width = tokens.shape
    local_experts = gate_up_weight.shape[0]
    size = lax.axis_size("expert")
    expert_count = local_experts * size
    half, mid = size // 2, rows // 2
    order = ring_order(size)
    forward = [(order[p], order[(p + 1) % size]) for p in range(size)]
    backward = [(b, a) for a, b in forward]
    me = lax.axis_index("expert")
    experts = jnp.arange(expert_count, dtype=jnp.int32)
    onehot = expert_ids[:, :, None] == experts[None, None, :]
    dense_gates = jnp.sum(
        jnp.where(onehot, gate_probs[:, :, None].astype(jnp.float32), 0.0), axis=1
    ).astype(jnp.bfloat16)
    gates = lax.all_to_all(dense_gates, "expert", split_axis=1, concat_axis=0, tiled=True)
    gates = gates.reshape(size, rows, local_experts)
    followers = [[order[(order.index(e) + k) % size] for k in range(size)] for e in range(size)]
    mine = lax.broadcasted_iota(jnp.int32, (size, size), 0) == me
    table = jnp.sum(jnp.where(mine, jnp.asarray(followers, jnp.int32), 0), axis=0)
    table = jnp.concatenate([table, me[None].astype(jnp.int32)])

    blocks = [(0, 0, rows, tokens, out_grad)]
    left, right = (tokens, out_grad), (tokens, out_grad)
    for step in range(1, half + 1):
        if step == half:
            left, right = tuple(a[:mid] for a in left), tuple(a[mid:] for a in right)
        xl = lax.ppermute(left[0], "expert", forward)
        xr = lax.ppermute(right[0], "expert", backward)
        left = (xl, lax.ppermute(left[1], "expert", forward))
        right = (xr, lax.ppermute(right[1], "expert", backward))
        if step < half:
            blocks.append((size - step, 0, rows) + left)
            blocks.append((step, 0, rows) + right)
    blocks.append((half, 0, mid) + left)
    blocks.append((half, mid, rows) + right)

    groups = [blocks[:3]] + [blocks[i : i + 2] for i in range(3, len(blocks), 2)]
    results = []
    for number, group in enumerate(groups):
        results.append(
            expert_blocks(group, table, gates, gate_up_weight, down_weight, number < half - 2)
        )
    partial_rows = [r for result in results[:-2] for r in result[2]]
    partial_rows += row_blocks(
        [r[0] for r in results[-2:]],
        [r[2][0] for r in results[-2:]],
        [rows, rows, mid, mid],
        gate_up_weight,
    )

    narrow = lambda a: a.astype(jnp.bfloat16)
    returned = []
    for stream in range(2):
        mine = [r.astype(jnp.float32) for r in partial_rows[stream::2]]
        to_left, to_right = partial_rows[stream - 4], partial_rows[stream - 2]
        for step in range(half - 1, -1, -1):
            from_right = lax.ppermute(to_left, "expert", backward).astype(jnp.float32)
            from_left = lax.ppermute(to_right, "expert", forward).astype(jnp.float32)
            if step == half - 1:
                pad = jnp.zeros((mid, from_left.shape[1]), jnp.float32)
                from_right = jnp.concatenate([from_right, pad])
                from_left = jnp.concatenate([pad, from_left])
            if step > 0:
                to_left = narrow(mine[2 * step - 1] + from_right)
                to_right = narrow(mine[2 * step] + from_left)
        returned.append(narrow(mine[0] + from_right + from_left))
    split = returned[0].shape[1]
    grad_tokens = jnp.concatenate([returned[0], returned[1][:, : width - split]], axis=1)
    probs = returned[1][:, width - split :][:, :expert_count].astype(jnp.float32)
    grad_probs = narrow(jnp.sum(jnp.where(onehot, probs[:, None, :], 0.0), axis=2))

    replicas = lax.axis_size("dp")
    outer = replicas // 2
    swap = [(i, i ^ 1) for i in range(replicas)]
    xs, gs = [b[3] for b in blocks], [b[4] for b in blocks]
    pres, hiddens = [r[0] for r in results], [r[1] for r in results]
    units = down_weight.shape[1]
    third = 2 * units // 3
    chunks = [(xs, pres, 0, 2 * third), (gs, hiddens, 0, units), (xs, pres, 2 * third, third)]
    places = [0, 2, 2]
    parts = []
    for chunk in chunks:
        parts += weight_parts(*chunk, replicas)
    weight_total = None
    for number, at in enumerate(places):
        sent, kept = parts[2 * number : 2 * number + 2]
        arrived = lax.ppermute(sent, "dp", swap)
        pieces = [kept, arrived]
        for shift in range(1, outer):
            pairs = [
                (2 * y + c, 2 * ((y + shift) % outer) + c) for y in range(outer) for c in range(2)
            ]
            both = kept[shift - 1].astype(jnp.float32) + arrived[shift - 1].astype(jnp.float32)
            pieces.append(lax.ppermute(narrow(both)[None], "dp", pairs))
        weight_total = place_chunk(pieces, at, local_experts, 3 * units, weight_total)
    return (grad_tokens, grad_probs, weight_total)


def solution(mesh):
    in_specs = (
        P(("dp", "expert"), None),
        P(("dp", "expert"), None),
        P(("dp", "expert"), None),
        P(("dp", "expert"), None),
        P("expert", None, None),
        P("expert", None, None),
    )
    out_specs = (P(("dp", "expert"), None), P(("dp", "expert"), None), P("dp", "expert", None))
    return jax.shard_map(layer, mesh=mesh, in_specs=in_specs, out_specs=out_specs, check_vma=False)
```

```python
import functools

import jax
import jax.numpy as jnp
from jax import lax
from jax.experimental import pallas as pl
from jax.experimental.pallas import tpu as pltpu
from jax.sharding import PartitionSpec as P


VMEM_BYTES = 67043328


def ring_order(size):
    half = size // 2
    return [2 * p if p < half else 2 * (size - 1 - p) + 1 for p in range(size)]


def joined(refs):
    parts = [ref[...] for ref in refs]
    return parts[0] if len(parts) == 1 else jnp.concatenate(parts, axis=0)


def expert_kernel(count, size, scalars, *refs):
    g_refs, gate_refs = refs[:count], refs[count : 2 * count]
    first, (w_in, w_out, pre_ref, hidden_ref) = 2 * count, refs[-(count + 5) : -(count + 1)]
    row_refs, total = refs[-(count + 1) : -1], refs[-1]
    e, last = pl.program_id(0), pl.num_programs(0) - 1
    units, width = w_out.shape[1:]
    x_refs = refs[first : -(count + 5)]
    pre = jnp.dot(joined(x_refs), w_in[0], preferred_element_type=jnp.float32)
    back = lax.dot_general(
        joined(g_refs), w_out[0], (((1,), (1,)), ((), ())), preferred_element_type=jnp.float32
    )
    gates = [ref[0].astype(jnp.float32) for ref in gate_refs]
    gates = gates[0] if count == 1 else jnp.concatenate(gates, axis=0)
    column = lax.broadcasted_iota(jnp.int32, gates.shape, 1) == e
    weight = jnp.sum(jnp.where(column, gates, 0.0), axis=1, keepdims=True)
    gate_pre, up_pre = pre[:, :units], pre[:, units:]
    logistic = 1.0 / (1.0 + jnp.exp(-gate_pre))
    active = gate_pre * logistic
    slope = logistic * (1.0 + gate_pre * (1.0 - logistic))
    hidden = (active * up_pre).astype(jnp.bfloat16).astype(jnp.float32)
    probs = jnp.sum(hidden * back, axis=1, keepdims=True)
    hidden_ref[0] = (weight * hidden).astype(jnp.bfloat16)
    grad_hidden = weight * back
    pre_ref[0, :, :units] = (grad_hidden * up_pre * slope).astype(jnp.bfloat16)
    pre_ref[0, :, units:] = (grad_hidden * active).astype(jnp.bfloat16)
    rows = lax.dot_general(
        pre_ref[0], w_in[0], (((1,), (1,)), ((), ())), preferred_element_type=jnp.float32
    )
    lane = lax.broadcasted_iota(jnp.int32, (rows.shape[0], total.shape[1] - width), 1)
    tail = jnp.where(lane == scalars[size] * pl.num_programs(0) + e, probs, 0.0)

    @pl.when(e == 0)
    def _():
        total[:, :width] = rows
        total[:, width:] = tail

    @pl.when(e > 0)
    def _():
        total[:, :width] += rows
        total[:, width:] += tail

    @pl.when(e == last)
    def _():
        at = 0
        for ref in row_refs:
            ref[...] = total[at : at + ref.shape[0]].astype(jnp.bfloat16)
            at += ref.shape[0]


def expert_blocks(blocks, table, gates, weight_in, weight_out):
    count = len(blocks)
    experts, width, wide = weight_in.shape
    units = weight_out.shape[1]
    sizes = [b[2] - b[1] for b in blocks]
    rows = sum(sizes)
    full = width + -(-gates.shape[0] * experts // 128) * 128
    whole = lambda n, w=width: pl.BlockSpec((n, w), lambda e, s: (0, 0))

    def gate_spec(offset, lo, n):
        return pl.BlockSpec((1, n, experts), lambda e, s: (s[offset], lo // n, 0))

    per_expert = lambda a, b: pl.BlockSpec((1, a, b), lambda e, s: (e, 0, 0))
    out = pl.pallas_call(
        functools.partial(expert_kernel, count, gates.shape[0]),
        out_shape=[
            jax.ShapeDtypeStruct((experts, rows, wide), jnp.bfloat16),
            jax.ShapeDtypeStruct((experts, rows, units), jnp.bfloat16),
        ]
        + [jax.ShapeDtypeStruct((n, full), jnp.bfloat16) for n in sizes],
        grid_spec=pltpu.PrefetchScalarGridSpec(
            num_scalar_prefetch=1,
            grid=(experts,),
            in_specs=[whole(n) for n in sizes]
            + [gate_spec(b[0], b[1], b[2] - b[1]) for b in blocks]
            + [whole(n) for n in sizes]
            + [per_expert(width, wide), per_expert(units, width)],
            out_specs=[per_expert(rows, wide), per_expert(rows, units)]
            + [whole(n, full) for n in sizes],
            scratch_shapes=[pltpu.VMEM((rows, full), jnp.float32)],
        ),
        cost_estimate=pl.CostEstimate(
            flops=2 * rows * experts * width * (2 * wide + units),
            bytes_accessed=2 * experts * width * (wide + units) + 8 * rows * width,
            transcendentals=0,
        ),
        compiler_params=pltpu.CompilerParams(vmem_limit_bytes=VMEM_BYTES),
        name="experts",
    )(table, *[b[4] for b in blocks], *[gates] * count, *[b[3] for b in blocks], weight_in, weight_out)
    return out[0], out[1], out[2:]


def weight_kernel(x_rows, p_rows, start, depth, *refs):
    x_refs, p_refs = refs[: len(x_rows)], refs[len(x_rows) : len(x_rows) + len(p_rows)]
    sent, kept, held, gradients, result, x_sems, p_sems, sems = refs[len(x_rows) + len(p_rows) :]
    outer, experts = sent.shape[0], p_refs[0].shape[0]
    size = sent.shape[2] // experts

    core, mine = lax.axis_index("dp") & 1, lax.axis_index("dp") >> 1

    def slabs(i):
        for place in range(outer):
            block = 2 * lax.rem(mine + 1 + place, outer) + (1 - core if i == 0 else core)
            column = pl.multiple_of(block * depth, depth)
            row = 0
            for k, n in enumerate(x_rows):
                yield pltpu.make_async_copy(
                    x_refs[k].at[:, pl.ds(column, depth)],
                    held.at[i, row : row + n, place * depth : (place + 1) * depth],
                    x_sems.at[i, place, k],
                )
                row += n

    def gradient_copies():
        row = 0
        for k, n in enumerate(p_rows):
            for e in range(experts):
                yield pltpu.make_async_copy(
                    p_refs[k].at[e, :, start : start + size],
                    gradients.at[row : row + n, e * size : (e + 1) * size],
                    p_sems.at[k, e],
                )
            row += n

    for copy in [*slabs(0), *gradient_copies(), *slabs(1)]:
        copy.start()
    for copy in gradient_copies():
        copy.wait()
    stores = []
    for i, out in enumerate((sent, kept)):
        for copy in slabs(i):
            copy.wait()
        part = lax.dot_general(
            held[i], gradients[...], (((0,), (0,)), ((), ())), preferred_element_type=jnp.float32
        )
        result[i] = part.astype(jnp.bfloat16).reshape(result.shape[1:])
        stores.append(pltpu.make_async_copy(result.at[i], out, sems.at[i]))
        stores[-1].start()
    for store in stores:
        store.wait()


def weight_parts(xs, ps, start, size, replicas):
    width = xs[0].shape[1]
    experts = ps[0].shape[0]
    outer, depth = replicas // 2, width // replicas
    x_rows, p_rows = [x.shape[0] for x in xs], [p.shape[1] for p in ps]
    rows, columns = sum(x_rows), experts * size

    anywhere = pl.BlockSpec(memory_space=pl.ANY)
    return pl.pallas_call(
        functools.partial(weight_kernel, x_rows, p_rows, start, depth),
        out_shape=[jax.ShapeDtypeStruct((outer, depth, columns), jnp.bfloat16)] * 2,
        in_specs=[anywhere] * (len(xs) + len(ps)),
        out_specs=[anywhere] * 2,
        scratch_shapes=[
            pltpu.VMEM((2, rows, outer * depth), jnp.bfloat16),
            pltpu.VMEM((rows, columns), jnp.bfloat16),
            pltpu.VMEM((2, outer, depth, columns), jnp.bfloat16),
            pltpu.SemaphoreType.DMA((2, outer, len(xs))),
            pltpu.SemaphoreType.DMA((len(ps), experts)),
            pltpu.SemaphoreType.DMA((2,)),
        ],
        cost_estimate=pl.CostEstimate(
            flops=2 * rows * width * columns,
            bytes_accessed=2 * (rows * (width + columns) + width * columns),
            transcendentals=0,
        ),
        name="weights",
    )(*xs, *ps)


def place_kernel(count, *refs):
    total = refs[0][...].astype(jnp.float32)
    for ref in refs[1:count]:
        total += ref[...].astype(jnp.float32)
    out = refs[-1]
    size = out.shape[2]
    for e in range(out.shape[1]):
        out[:, e, :] = total[:, e * size : (e + 1) * size].astype(jnp.bfloat16)


def place_chunk(pieces, at, experts, columns, held=None):
    depth, size = pieces[0].shape[1], pieces[0].shape[2] // experts
    tile = depth
    specs = [
        pl.BlockSpec((None, tile, experts * size), lambda i, last=p.shape[0] - 1: (last, i, 0))
        for p in pieces
    ]
    args = list(pieces) + ([] if held is None else [held])
    return pl.pallas_call(
        functools.partial(place_kernel, len(pieces)),
        out_shape=jax.ShapeDtypeStruct((depth, experts, columns), jnp.bfloat16),
        grid=(depth // tile,),
        in_specs=specs
        + ([] if held is None else [pl.BlockSpec(memory_space=pl.ANY)]),
        out_specs=pl.BlockSpec((tile, experts, size), lambda i: (i, 0, at)),
        input_output_aliases={} if held is None else {len(pieces): 0},
        compiler_params=pltpu.CompilerParams(vmem_limit_bytes=VMEM_BYTES),
        name="place",
    )(*args)


def layer(tokens, out_grad, expert_ids, gate_probs, gate_up_weight, down_weight):
    rows, width = tokens.shape
    local_experts = gate_up_weight.shape[0]
    size = lax.axis_size("expert")
    expert_count = local_experts * size
    half, mid = size // 2, rows // 2
    order = ring_order(size)
    forward = [(order[p], order[(p + 1) % size]) for p in range(size)]
    backward = [(b, a) for a, b in forward]
    me = lax.axis_index("expert")
    experts = jnp.arange(expert_count, dtype=jnp.int32)
    onehot = expert_ids[:, :, None] == experts[None, None, :]
    dense_gates = jnp.sum(
        jnp.where(onehot, gate_probs[:, :, None].astype(jnp.float32), 0.0), axis=1
    ).astype(jnp.bfloat16)
    gates = lax.all_to_all(dense_gates, "expert", split_axis=1, concat_axis=0, tiled=True)
    gates = gates.reshape(size, rows, local_experts)
    followers = [[order[(order.index(e) + k) % size] for k in range(size)] for e in range(size)]
    mine = lax.broadcasted_iota(jnp.int32, (size, size), 0) == me
    table = jnp.sum(jnp.where(mine, jnp.asarray(followers, jnp.int32), 0), axis=0)
    table = jnp.concatenate([table, me[None].astype(jnp.int32)])

    blocks = [(0, 0, rows, tokens, out_grad)]
    left, right = (tokens, out_grad), (tokens, out_grad)
    for step in range(1, half + 1):
        if step == half:
            left, right = tuple(a[:mid] for a in left), tuple(a[mid:] for a in right)
        xl = lax.ppermute(left[0], "expert", forward)
        xr = lax.ppermute(right[0], "expert", backward)
        left = (xl, lax.ppermute(left[1], "expert", forward))
        right = (xr, lax.ppermute(right[1], "expert", backward))
        if step < half:
            blocks.append((size - step, 0, rows) + left)
            blocks.append((step, 0, rows) + right)
    blocks.append((half, 0, mid) + left)
    blocks.append((half, mid, rows) + right)

    groups = [blocks[:3]] + [blocks[i : i + 2] for i in range(3, len(blocks), 2)]
    results = []
    for group in groups:
        results.append(
            expert_blocks(group, table, gates, gate_up_weight, down_weight)
        )
    partial_rows = [r for result in results for r in result[2]]

    narrow = lambda a: a.astype(jnp.bfloat16)
    to_left, to_right = partial_rows[-2], partial_rows[-1]
    for step in range(half - 1, -1, -1):
        from_right = lax.ppermute(to_left, "expert", backward).astype(jnp.float32)
        from_left = lax.ppermute(to_right, "expert", forward).astype(jnp.float32)
        if step == half - 1:
            pad = jnp.zeros((mid, from_left.shape[1]), jnp.float32)
            from_right = jnp.concatenate([from_right, pad])
            from_left = jnp.concatenate([pad, from_left])
        if step > 0:
            to_left = narrow(partial_rows[2 * step - 1].astype(jnp.float32) + from_right)
            to_right = narrow(partial_rows[2 * step].astype(jnp.float32) + from_left)
    returned = narrow(partial_rows[0].astype(jnp.float32) + from_right + from_left)
    grad_tokens = returned[:, :width]
    probs = returned[:, width : width + expert_count].astype(jnp.float32)
    grad_probs = narrow(jnp.sum(jnp.where(onehot, probs[:, None, :], 0.0), axis=2))

    replicas = lax.axis_size("dp")
    outer = replicas // 2
    swap = [(i, i ^ 1) for i in range(replicas)]
    xs, gs = [b[3] for b in blocks], [b[4] for b in blocks]
    pres, hiddens = [r[0] for r in results], [r[1] for r in results]
    units = down_weight.shape[1]
    chunks = [(xs, pres, 0, units), (gs, hiddens, 0, units), (xs, pres, units, units)]
    places = [0, 2, 1]
    parts = []
    for chunk in chunks:
        parts += weight_parts(*chunk, replicas)
    weight_total = None
    for number, at in enumerate(places):
        sent, kept = parts[2 * number : 2 * number + 2]
        arrived = lax.ppermute(sent, "dp", swap)
        pieces = [kept, arrived]
        for shift in range(1, outer):
            pairs = [
                (2 * y + c, 2 * ((y + shift) % outer) + c) for y in range(outer) for c in range(2)
            ]
            both = kept[shift - 1].astype(jnp.float32) + arrived[shift - 1].astype(jnp.float32)
            pieces.append(lax.ppermute(narrow(both)[None], "dp", pairs))
        weight_total = place_chunk(pieces, at, local_experts, 3 * units, weight_total)
    return (grad_tokens, grad_probs, weight_total)


def solution(mesh):
    in_specs = (
        P(("dp", "expert"), None),
        P(("dp", "expert"), None),
        P(("dp", "expert"), None),
        P(("dp", "expert"), None),
        P("expert", None, None),
        P("expert", None, None),
    )
    out_specs = (P(("dp", "expert"), None), P(("dp", "expert"), None), P("dp", "expert", None))
    return jax.shard_map(layer, mesh=mesh, in_specs=in_specs, out_specs=out_specs, check_vma=False)
```

```python
import functools

import jax
import jax.numpy as jnp
from jax import lax
from jax.experimental import pallas as pl
from jax.experimental.pallas import tpu as pltpu
from jax.sharding import PartitionSpec as P


VMEM_BYTES = 67043328


def ring_order(size):
    half = size // 2
    return [2 * p if p < half else 2 * (size - 1 - p) + 1 for p in range(size)]


def joined(refs):
    parts = [ref[...] for ref in refs]
    return parts[0] if len(parts) == 1 else jnp.concatenate(parts, axis=0)


def expert_kernel(count, size, scalars, *refs):
    g_refs, gate_refs = refs[:count], refs[count : 2 * count]
    first, (w_in, w_out, pre_ref, hidden_ref) = 2 * count, refs[-(count + 5) : -(count + 1)]
    row_refs, total = refs[-(count + 1) : -1], refs[-1]
    e, last = pl.program_id(0), pl.num_programs(0) - 1
    units, width = w_out.shape[1:]
    x_refs = refs[first : -(count + 5)]
    pre = jnp.dot(joined(x_refs), w_in[0], preferred_element_type=jnp.float32)
    back = lax.dot_general(
        joined(g_refs), w_out[0], (((1,), (1,)), ((), ())), preferred_element_type=jnp.float32
    )
    gates = [ref[0].astype(jnp.float32) for ref in gate_refs]
    gates = gates[0] if count == 1 else jnp.concatenate(gates, axis=0)
    column = lax.broadcasted_iota(jnp.int32, gates.shape, 1) == e
    weight = jnp.sum(jnp.where(column, gates, 0.0), axis=1, keepdims=True)
    gate_pre, up_pre = pre[:, :units], pre[:, units:]
    logistic = 1.0 / (1.0 + jnp.exp(-gate_pre))
    active = gate_pre * logistic
    slope = logistic * (1.0 + gate_pre * (1.0 - logistic))
    hidden = (active * up_pre).astype(jnp.bfloat16).astype(jnp.float32)
    probs = jnp.sum(hidden * back, axis=1, keepdims=True)
    hidden_ref[0] = (weight * hidden).astype(jnp.bfloat16)
    grad_hidden = weight * back
    pre_ref[0, :, :units] = (grad_hidden * up_pre * slope).astype(jnp.bfloat16)
    pre_ref[0, :, units:] = (grad_hidden * active).astype(jnp.bfloat16)
    rows = lax.dot_general(
        pre_ref[0], w_in[0], (((1,), (1,)), ((), ())), preferred_element_type=jnp.float32
    )
    lane = lax.broadcasted_iota(jnp.int32, (rows.shape[0], total.shape[1] - width), 1)
    tail = jnp.where(lane == scalars[size] * pl.num_programs(0) + e, probs, 0.0)

    @pl.when(e == 0)
    def _():
        total[:, :width] = rows
        total[:, width:] = tail

    @pl.when(e > 0)
    def _():
        total[:, :width] += rows
        total[:, width:] += tail

    @pl.when(e == last)
    def _():
        at = 0
        for ref in row_refs:
            ref[...] = total[at : at + ref.shape[0]].astype(jnp.bfloat16)
            at += ref.shape[0]


def expert_blocks(blocks, table, gates, weight_in, weight_out, vmem):
    count = len(blocks)
    experts, width, wide = weight_in.shape
    units = weight_out.shape[1]
    sizes = [b[2] - b[1] for b in blocks]
    rows = sum(sizes)
    full = width + -(-gates.shape[0] * experts // 128) * 128
    whole = lambda n, w=width: pl.BlockSpec((n, w), lambda e, s: (0, 0))

    def gate_spec(offset, lo, n):
        return pl.BlockSpec((1, n, experts), lambda e, s: (s[offset], lo // n, 0))

    per_expert = lambda a, b: pl.BlockSpec((1, a, b), lambda e, s: (e, 0, 0))
    out = pl.pallas_call(
        functools.partial(expert_kernel, count, gates.shape[0]),
        out_shape=[
            jax.ShapeDtypeStruct((experts, rows, wide), jnp.bfloat16),
            jax.ShapeDtypeStruct((experts, rows, units), jnp.bfloat16),
        ]
        + [jax.ShapeDtypeStruct((n, full), jnp.bfloat16) for n in sizes],
        grid_spec=pltpu.PrefetchScalarGridSpec(
            num_scalar_prefetch=1,
            grid=(experts,),
            in_specs=[whole(n) for n in sizes]
            + [gate_spec(b[0], b[1], b[2] - b[1]) for b in blocks]
            + [whole(n) for n in sizes]
            + [per_expert(width, wide), per_expert(units, width)],
            out_specs=[per_expert(rows, wide), per_expert(rows, units)]
            + [whole(n, full) for n in sizes],
            scratch_shapes=[pltpu.VMEM((rows, full), jnp.float32)],
        ),
        cost_estimate=pl.CostEstimate(
            flops=2 * rows * experts * width * (2 * wide + units),
            bytes_accessed=2 * experts * width * (wide + units) + 8 * rows * width,
            transcendentals=0,
        ),
        compiler_params=pltpu.CompilerParams(vmem_limit_bytes=vmem),
        name="experts",
    )(table, *[b[4] for b in blocks], *[gates] * count, *[b[3] for b in blocks], weight_in, weight_out)
    return out[0], out[1], out[2:]


def weight_kernel(x_rows, p_rows, start, depth, *refs):
    x_refs, p_refs = refs[: len(x_rows)], refs[len(x_rows) : len(x_rows) + len(p_rows)]
    sent, kept, held, gradients, result, x_sems, p_sems, sems = refs[len(x_rows) + len(p_rows) :]
    outer, experts = sent.shape[0], p_refs[0].shape[0]
    size = sent.shape[2] // experts

    core, mine = lax.axis_index("dp") & 1, lax.axis_index("dp") >> 1

    def slabs(i):
        for place in range(outer):
            block = 2 * lax.rem(mine + 1 + place, outer) + (1 - core if i == 0 else core)
            column = pl.multiple_of(block * depth, depth)
            row = 0
            for k, n in enumerate(x_rows):
                yield pltpu.make_async_copy(
                    x_refs[k].at[:, pl.ds(column, depth)],
                    held.at[i, row : row + n, place * depth : (place + 1) * depth],
                    x_sems.at[i, place, k],
                )
                row += n

    def gradient_copies():
        row = 0
        for k, n in enumerate(p_rows):
            for e in range(experts):
                yield pltpu.make_async_copy(
                    p_refs[k].at[e, :, start : start + size],
                    gradients.at[row : row + n, e * size : (e + 1) * size],
                    p_sems.at[k, e],
                )
            row += n

    for copy in [*slabs(0), *gradient_copies(), *slabs(1)]:
        copy.start()
    for copy in gradient_copies():
        copy.wait()
    stores = []
    for i, out in enumerate((sent, kept)):
        for copy in slabs(i):
            copy.wait()
        part = lax.dot_general(
            held[i], gradients[...], (((0,), (0,)), ((), ())), preferred_element_type=jnp.float32
        )
        result[i] = part.astype(jnp.bfloat16).reshape(result.shape[1:])
        stores.append(pltpu.make_async_copy(result.at[i], out, sems.at[i]))
        stores[-1].start()
    for store in stores:
        store.wait()


def weight_parts(xs, ps, start, size, replicas):
    width = xs[0].shape[1]
    experts = ps[0].shape[0]
    outer, depth = replicas // 2, width // replicas
    x_rows, p_rows = [x.shape[0] for x in xs], [p.shape[1] for p in ps]
    rows, columns = sum(x_rows), experts * size

    anywhere = pl.BlockSpec(memory_space=pl.ANY)
    return pl.pallas_call(
        functools.partial(weight_kernel, x_rows, p_rows, start, depth),
        out_shape=[jax.ShapeDtypeStruct((outer, depth, columns), jnp.bfloat16)] * 2,
        in_specs=[anywhere] * (len(xs) + len(ps)),
        out_specs=[anywhere] * 2,
        scratch_shapes=[
            pltpu.VMEM((2, rows, outer * depth), jnp.bfloat16),
            pltpu.VMEM((rows, columns), jnp.bfloat16),
            pltpu.VMEM((2, outer, depth, columns), jnp.bfloat16),
            pltpu.SemaphoreType.DMA((2, outer, len(xs))),
            pltpu.SemaphoreType.DMA((len(ps), experts)),
            pltpu.SemaphoreType.DMA((2,)),
        ],
        cost_estimate=pl.CostEstimate(
            flops=2 * rows * width * columns,
            bytes_accessed=2 * (rows * (width + columns) + width * columns),
            transcendentals=0,
        ),
        name="weights",
    )(*xs, *ps)


def place_kernel(count, *refs):
    total = refs[0][...].astype(jnp.float32)
    for ref in refs[1:count]:
        total += ref[...].astype(jnp.float32)
    out = refs[-1]
    size = out.shape[2]
    for e in range(out.shape[1]):
        out[:, e, :] = total[:, e * size : (e + 1) * size].astype(jnp.bfloat16)


def place_chunk(pieces, at, experts, columns, held=None):
    depth, size = pieces[0].shape[1], pieces[0].shape[2] // experts
    tile = depth
    specs = [
        pl.BlockSpec((None, tile, experts * size), lambda i, last=p.shape[0] - 1: (last, i, 0))
        for p in pieces
    ]
    args = list(pieces) + ([] if held is None else [held])
    return pl.pallas_call(
        functools.partial(place_kernel, len(pieces)),
        out_shape=jax.ShapeDtypeStruct((depth, experts, columns), jnp.bfloat16),
        grid=(depth // tile,),
        in_specs=specs
        + ([] if held is None else [pl.BlockSpec(memory_space=pl.ANY)]),
        out_specs=pl.BlockSpec((tile, experts, size), lambda i: (i, 0, at)),
        input_output_aliases={} if held is None else {len(pieces): 0},
        compiler_params=pltpu.CompilerParams(vmem_limit_bytes=VMEM_BYTES),
        name="place",
    )(*args)


def layer(tokens, out_grad, expert_ids, gate_probs, gate_up_weight, down_weight):
    rows, width = tokens.shape
    local_experts = gate_up_weight.shape[0]
    size = lax.axis_size("expert")
    expert_count = local_experts * size
    half, mid = size // 2, rows // 2
    order = ring_order(size)
    forward = [(order[p], order[(p + 1) % size]) for p in range(size)]
    backward = [(b, a) for a, b in forward]
    me = lax.axis_index("expert")
    experts = jnp.arange(expert_count, dtype=jnp.int32)
    onehot = expert_ids[:, :, None] == experts[None, None, :]
    dense_gates = jnp.sum(
        jnp.where(onehot, gate_probs[:, :, None].astype(jnp.float32), 0.0), axis=1
    ).astype(jnp.bfloat16)
    gates = lax.all_to_all(dense_gates, "expert", split_axis=1, concat_axis=0, tiled=True)
    gates = gates.reshape(size, rows, local_experts)
    followers = [[order[(order.index(e) + k) % size] for k in range(size)] for e in range(size)]
    mine = lax.broadcasted_iota(jnp.int32, (size, size), 0) == me
    table = jnp.sum(jnp.where(mine, jnp.asarray(followers, jnp.int32), 0), axis=0)
    table = jnp.concatenate([table, me[None].astype(jnp.int32)])

    blocks = [(0, 0, rows, tokens, out_grad)]
    left, right = (tokens, out_grad), (tokens, out_grad)
    for step in range(1, half + 1):
        if step == half:
            left, right = tuple(a[:mid] for a in left), tuple(a[mid:] for a in right)
        xl = lax.ppermute(left[0], "expert", forward)
        xr = lax.ppermute(right[0], "expert", backward)
        left = (xl, lax.ppermute(left[1], "expert", forward))
        right = (xr, lax.ppermute(right[1], "expert", backward))
        if step < half:
            blocks.append((size - step, 0, rows) + left)
            blocks.append((step, 0, rows) + right)
    blocks.append((half, 0, mid) + left)
    blocks.append((half, mid, rows) + right)

    groups = [blocks[:3]] + [blocks[i : i + 2] for i in range(3, len(blocks), 2)]
    results = []
    for number, group in enumerate(groups):
        results.append(
            expert_blocks(
                group, table, gates, gate_up_weight, down_weight,
                VMEM_BYTES if number == half - 1 else None,
            )
        )
    partial_rows = [r for result in results for r in result[2]]

    narrow = lambda a: a.astype(jnp.bfloat16)
    to_left, to_right = partial_rows[-2], partial_rows[-1]
    for step in range(half - 1, -1, -1):
        from_right = lax.ppermute(to_left, "expert", backward).astype(jnp.float32)
        from_left = lax.ppermute(to_right, "expert", forward).astype(jnp.float32)
        if step == half - 1:
            pad = jnp.zeros((mid, from_left.shape[1]), jnp.float32)
            from_right = jnp.concatenate([from_right, pad])
            from_left = jnp.concatenate([pad, from_left])
        if step > 0:
            to_left = narrow(partial_rows[2 * step - 1].astype(jnp.float32) + from_right)
            to_right = narrow(partial_rows[2 * step].astype(jnp.float32) + from_left)
    returned = narrow(partial_rows[0].astype(jnp.float32) + from_right + from_left)
    grad_tokens = returned[:, :width]
    probs = returned[:, width : width + expert_count].astype(jnp.float32)
    grad_probs = narrow(jnp.sum(jnp.where(onehot, probs[:, None, :], 0.0), axis=2))

    replicas = lax.axis_size("dp")
    outer = replicas // 2
    swap = [(i, i ^ 1) for i in range(replicas)]
    xs, gs = [b[3] for b in blocks], [b[4] for b in blocks]
    pres, hiddens = [r[0] for r in results], [r[1] for r in results]
    units = down_weight.shape[1]
    chunks = [(xs, pres, 0, units), (gs, hiddens, 0, units), (xs, pres, units, units)]
    places = [0, 2, 1]
    parts = []
    for chunk in chunks:
        parts += weight_parts(*chunk, replicas)
    weight_total = None
    for number, at in enumerate(places):
        sent, kept = parts[2 * number : 2 * number + 2]
        arrived = lax.ppermute(sent, "dp", swap)
        pieces = [kept, arrived]
        for shift in range(1, outer):
            pairs = [
                (2 * y + c, 2 * ((y + shift) % outer) + c) for y in range(outer) for c in range(2)
            ]
            both = kept[shift - 1].astype(jnp.float32) + arrived[shift - 1].astype(jnp.float32)
            pieces.append(lax.ppermute(narrow(both)[None], "dp", pairs))
        weight_total = place_chunk(pieces, at, local_experts, 3 * units, weight_total)
    return (grad_tokens, grad_probs, weight_total)


def solution(mesh):
    in_specs = (
        P(("dp", "expert"), None),
        P(("dp", "expert"), None),
        P(("dp", "expert"), None),
        P(("dp", "expert"), None),
        P("expert", None, None),
        P("expert", None, None),
    )
    out_specs = (P(("dp", "expert"), None), P(("dp", "expert"), None), P("dp", "expert", None))
    return jax.shard_map(layer, mesh=mesh, in_specs=in_specs, out_specs=out_specs, check_vma=False)
```

```python
import functools

import jax
import jax.numpy as jnp
from jax import lax
from jax.experimental import pallas as pl
from jax.experimental.pallas import tpu as pltpu
from jax.sharding import PartitionSpec as P


VMEM_BYTES = 67043328


def ring_order(size):
    half = size // 2
    return [2 * p if p < half else 2 * (size - 1 - p) + 1 for p in range(size)]


def joined(refs):
    parts = [ref[...] for ref in refs]
    return parts[0] if len(parts) == 1 else jnp.concatenate(parts, axis=0)


def expert_kernel(count, size, scalars, *refs):
    g_refs, gate_refs = refs[:count], refs[count : 2 * count]
    first, (w_in, w_out, pre_ref, hidden_ref) = 2 * count, refs[-(count + 5) : -(count + 1)]
    row_refs, total = refs[-(count + 1) : -1], refs[-1]
    e, last = pl.program_id(0), pl.num_programs(0) - 1
    units, width = w_out.shape[1:]
    x_refs = refs[first : -(count + 5)]
    pre = jnp.dot(joined(x_refs), w_in[0], preferred_element_type=jnp.float32)
    back = lax.dot_general(
        joined(g_refs), w_out[0], (((1,), (1,)), ((), ())), preferred_element_type=jnp.float32
    )
    gates = [ref[0].astype(jnp.float32) for ref in gate_refs]
    gates = gates[0] if count == 1 else jnp.concatenate(gates, axis=0)
    column = lax.broadcasted_iota(jnp.int32, gates.shape, 1) == e
    weight = jnp.sum(jnp.where(column, gates, 0.0), axis=1, keepdims=True)
    gate_pre, up_pre = pre[:, :units], pre[:, units:]
    logistic = 1.0 / (1.0 + jnp.exp(-gate_pre))
    active = gate_pre * logistic
    slope = logistic * (1.0 + gate_pre * (1.0 - logistic))
    hidden = (active * up_pre).astype(jnp.bfloat16).astype(jnp.float32)
    probs = jnp.sum(hidden * back, axis=1, keepdims=True)
    hidden_ref[0] = (weight * hidden).astype(jnp.bfloat16)
    grad_hidden = weight * back
    pre_ref[0, :, :units] = (grad_hidden * up_pre * slope).astype(jnp.bfloat16)
    pre_ref[0, :, units:] = (grad_hidden * active).astype(jnp.bfloat16)
    rows = lax.dot_general(
        pre_ref[0], w_in[0], (((1,), (1,)), ((), ())), preferred_element_type=jnp.float32
    )
    lane = lax.broadcasted_iota(jnp.int32, (rows.shape[0], total.shape[1] - width), 1)
    tail = jnp.where(lane == scalars[size] * pl.num_programs(0) + e, probs, 0.0)

    @pl.when(e == 0)
    def _():
        total[:, :width] = rows
        total[:, width:] = tail

    @pl.when(e > 0)
    def _():
        total[:, :width] += rows
        total[:, width:] += tail

    @pl.when(e == last)
    def _():
        at = 0
        for ref in row_refs:
            ref[...] = total[at : at + ref.shape[0]].astype(jnp.bfloat16)
            at += ref.shape[0]


def expert_blocks(blocks, table, gates, weight_in, weight_out, vmem):
    count = len(blocks)
    experts, width, wide = weight_in.shape
    units = weight_out.shape[1]
    sizes = [b[2] - b[1] for b in blocks]
    rows = sum(sizes)
    full = width + -(-gates.shape[0] * experts // 128) * 128
    whole = lambda n, w=width: pl.BlockSpec((n, w), lambda e, s: (0, 0))

    def gate_spec(offset, lo, n):
        return pl.BlockSpec((1, n, experts), lambda e, s: (s[offset], lo // n, 0))

    per_expert = lambda a, b: pl.BlockSpec((1, a, b), lambda e, s: (e, 0, 0))
    out = pl.pallas_call(
        functools.partial(expert_kernel, count, gates.shape[0]),
        out_shape=[
            jax.ShapeDtypeStruct((experts, rows, wide), jnp.bfloat16),
            jax.ShapeDtypeStruct((experts, rows, units), jnp.bfloat16),
        ]
        + [jax.ShapeDtypeStruct((n, full), jnp.bfloat16) for n in sizes],
        grid_spec=pltpu.PrefetchScalarGridSpec(
            num_scalar_prefetch=1,
            grid=(experts,),
            in_specs=[whole(n) for n in sizes]
            + [gate_spec(b[0], b[1], b[2] - b[1]) for b in blocks]
            + [whole(n) for n in sizes]
            + [per_expert(width, wide), per_expert(units, width)],
            out_specs=[per_expert(rows, wide), per_expert(rows, units)]
            + [whole(n, full) for n in sizes],
            scratch_shapes=[pltpu.VMEM((rows, full), jnp.float32)],
        ),
        cost_estimate=pl.CostEstimate(
            flops=2 * rows * experts * width * (2 * wide + units),
            bytes_accessed=2 * experts * width * (wide + units) + 8 * rows * width,
            transcendentals=0,
        ),
        compiler_params=pltpu.CompilerParams(vmem_limit_bytes=vmem),
        name="experts",
    )(table, *[b[4] for b in blocks], *[gates] * count, *[b[3] for b in blocks], weight_in, weight_out)
    return out[0], out[1], out[2:]


def begun_kernel(nx, *refs):
    p_refs = refs[nx:-1]
    experts = p_refs[0].shape[0]
    right = [jnp.concatenate([ref[e] for ref in p_refs], axis=0) for e in range(experts)]
    refs[-1][...] = lax.dot_general(
        joined(refs[:nx]),
        jnp.concatenate(right, axis=1),
        (((0,), (0,)), ((), ())),
        preferred_element_type=jnp.float32,
    ).astype(jnp.bfloat16)


def begun_weights(xs, ps, size):
    width, experts = xs[0].shape[1], ps[0].shape[0]
    depth, columns = width // 4, experts * size
    rows = sum(x.shape[0] for x in xs)
    return pl.pallas_call(
        functools.partial(begun_kernel, len(xs)),
        out_shape=jax.ShapeDtypeStruct((width, columns), jnp.bfloat16),
        grid=(width // depth,),
        in_specs=[pl.BlockSpec((x.shape[0], depth), lambda i: (0, i)) for x in xs]
        + [pl.BlockSpec((experts, p.shape[1], size), lambda i: (0, 0, 0)) for p in ps],
        out_specs=pl.BlockSpec((depth, columns), lambda i: (i, 0)),
        cost_estimate=pl.CostEstimate(
            flops=2 * rows * width * columns,
            bytes_accessed=2 * (rows * (width + columns) + width * columns),
            transcendentals=0,
        ),
        name="begun",
    )(*xs, *ps)


def weight_kernel(x_rows, p_rows, start, depth, begun_count, *refs):
    x_refs, p_refs = refs[: len(x_rows)], refs[len(x_rows) : len(x_rows) + len(p_rows)]
    begun = refs[len(x_rows) + len(p_rows) :][:begun_count]
    refs = refs[len(x_rows) + len(p_rows) + begun_count :]
    sent, kept, held, gradients, result, x_sems, p_sems, sems = refs[:8]
    outer, experts = sent.shape[0], p_refs[0].shape[0]
    size = sent.shape[2] // experts

    core, mine = lax.axis_index("dp") & 1, lax.axis_index("dp") >> 1

    def slabs(i):
        for place in range(outer):
            block = 2 * lax.rem(mine + 1 + place, outer) + (1 - core if i == 0 else core)
            column = pl.multiple_of(block * depth, depth)
            row = 0
            for k, n in enumerate(x_rows):
                yield pltpu.make_async_copy(
                    x_refs[k].at[:, pl.ds(column, depth)],
                    held.at[i, row : row + n, place * depth : (place + 1) * depth],
                    x_sems.at[i, place, k],
                )
                row += n
            for ref in begun:
                yield pltpu.make_async_copy(
                    ref.at[pl.ds(column, depth), :], refs[8].at[i, place], refs[9].at[i, place]
                )

    def gradient_copies():
        row = 0
        for k, n in enumerate(p_rows):
            for e in range(experts):
                yield pltpu.make_async_copy(
                    p_refs[k].at[e, :, start : start + size],
                    gradients.at[row : row + n, e * size : (e + 1) * size],
                    p_sems.at[k, e],
                )
            row += n

    for copy in [*slabs(0), *gradient_copies(), *slabs(1)]:
        copy.start()
    for copy in gradient_copies():
        copy.wait()
    stores = []
    for i, out in enumerate((sent, kept)):
        for copy in slabs(i):
            copy.wait()
        part = lax.dot_general(
            held[i], gradients[...], (((0,), (0,)), ((), ())), preferred_element_type=jnp.float32
        )
        part = part.reshape(result.shape[1:])
        if begun:
            part += refs[8][i].astype(jnp.float32)
        result[i] = part.astype(jnp.bfloat16)
        stores.append(pltpu.make_async_copy(result.at[i], out, sems.at[i]))
        stores[-1].start()
    for store in stores:
        store.wait()


def weight_parts(xs, ps, start, size, replicas, *begun):
    width = xs[0].shape[1]
    experts = ps[0].shape[0]
    outer, depth = replicas // 2, width // replicas
    x_rows, p_rows = [x.shape[0] for x in xs], [p.shape[1] for p in ps]
    rows, columns = sum(x_rows), experts * size

    anywhere = pl.BlockSpec(memory_space=pl.ANY)
    return pl.pallas_call(
        functools.partial(weight_kernel, x_rows, p_rows, start, depth, len(begun)),
        out_shape=[jax.ShapeDtypeStruct((outer, depth, columns), jnp.bfloat16)] * 2,
        in_specs=[anywhere] * (len(xs) + len(ps) + len(begun)),
        out_specs=[anywhere] * 2,
        scratch_shapes=[
            pltpu.VMEM((2, rows, outer * depth), jnp.bfloat16),
            pltpu.VMEM((rows, columns), jnp.bfloat16),
            pltpu.VMEM((2, outer, depth, columns), jnp.bfloat16),
            pltpu.SemaphoreType.DMA((2, outer, len(xs))),
            pltpu.SemaphoreType.DMA((len(ps), experts)),
            pltpu.SemaphoreType.DMA((2,)),
        ]
        + [
            pltpu.VMEM((2, outer, depth, columns), jnp.bfloat16),
            pltpu.SemaphoreType.DMA((2, outer)),
        ]
        * len(begun),
        cost_estimate=pl.CostEstimate(
            flops=2 * rows * width * columns,
            bytes_accessed=2 * (rows * (width + columns) + width * columns),
            transcendentals=0,
        ),
        name="weights",
    )(*xs, *ps, *begun)


def place_kernel(count, *refs):
    total = refs[0][...].astype(jnp.float32)
    for ref in refs[1:count]:
        total += ref[...].astype(jnp.float32)
    out = refs[-1]
    size = out.shape[2]
    for e in range(out.shape[1]):
        out[:, e, :] = total[:, e * size : (e + 1) * size].astype(jnp.bfloat16)


def place_chunk(pieces, at, experts, columns, held=None):
    depth, size = pieces[0].shape[1], pieces[0].shape[2] // experts
    tile = depth
    specs = [
        pl.BlockSpec((None, tile, experts * size), lambda i, last=p.shape[0] - 1: (last, i, 0))
        for p in pieces
    ]
    args = list(pieces) + ([] if held is None else [held])
    return pl.pallas_call(
        functools.partial(place_kernel, len(pieces)),
        out_shape=jax.ShapeDtypeStruct((depth, experts, columns), jnp.bfloat16),
        grid=(depth // tile,),
        in_specs=specs
        + ([] if held is None else [pl.BlockSpec(memory_space=pl.ANY)]),
        out_specs=pl.BlockSpec((tile, experts, size), lambda i: (i, 0, at)),
        input_output_aliases={} if held is None else {len(pieces): 0},
        compiler_params=pltpu.CompilerParams(vmem_limit_bytes=VMEM_BYTES),
        name="place",
    )(*args)


def layer(tokens, out_grad, expert_ids, gate_probs, gate_up_weight, down_weight):
    rows, width = tokens.shape
    local_experts = gate_up_weight.shape[0]
    size = lax.axis_size("expert")
    expert_count = local_experts * size
    half, mid = size // 2, rows // 2
    order = ring_order(size)
    forward = [(order[p], order[(p + 1) % size]) for p in range(size)]
    backward = [(b, a) for a, b in forward]
    me = lax.axis_index("expert")
    experts = jnp.arange(expert_count, dtype=jnp.int32)
    onehot = expert_ids[:, :, None] == experts[None, None, :]
    dense_gates = jnp.sum(
        jnp.where(onehot, gate_probs[:, :, None].astype(jnp.float32), 0.0), axis=1
    ).astype(jnp.bfloat16)
    gates = lax.all_to_all(dense_gates, "expert", split_axis=1, concat_axis=0, tiled=True)
    gates = gates.reshape(size, rows, local_experts)
    followers = [[order[(order.index(e) + k) % size] for k in range(size)] for e in range(size)]
    mine = lax.broadcasted_iota(jnp.int32, (size, size), 0) == me
    table = jnp.sum(jnp.where(mine, jnp.asarray(followers, jnp.int32), 0), axis=0)
    table = jnp.concatenate([table, me[None].astype(jnp.int32)])

    blocks = [(0, 0, rows, tokens, out_grad)]
    left, right = (tokens, out_grad), (tokens, out_grad)
    for step in range(1, half + 1):
        if step == half:
            left, right = tuple(a[:mid] for a in left), tuple(a[mid:] for a in right)
        xl = lax.ppermute(left[0], "expert", forward)
        xr = lax.ppermute(right[0], "expert", backward)
        left = (xl, lax.ppermute(left[1], "expert", forward))
        right = (xr, lax.ppermute(right[1], "expert", backward))
        if step < half:
            blocks.append((size - step, 0, rows) + left)
            blocks.append((step, 0, rows) + right)
    blocks.append((half, 0, mid) + left)
    blocks.append((half, mid, rows) + right)

    groups = [blocks[:3]] + [blocks[i : i + 2] for i in range(3, len(blocks), 2)]
    results = []
    for number, group in enumerate(groups):
        results.append(
            expert_blocks(
                group, table, gates, gate_up_weight, down_weight,
                VMEM_BYTES if number == half - 1 else None,
            )
        )
    partial_rows = [r for result in results for r in result[2]]

    narrow = lambda a: a.astype(jnp.bfloat16)
    to_left, to_right = partial_rows[-2], partial_rows[-1]
    for step in range(half - 1, -1, -1):
        from_right = lax.ppermute(to_left, "expert", backward).astype(jnp.float32)
        from_left = lax.ppermute(to_right, "expert", forward).astype(jnp.float32)
        if step == half - 1:
            pad = jnp.zeros((mid, from_left.shape[1]), jnp.float32)
            from_right = jnp.concatenate([from_right, pad])
            from_left = jnp.concatenate([pad, from_left])
        if step > 0:
            to_left = narrow(partial_rows[2 * step - 1].astype(jnp.float32) + from_right)
            to_right = narrow(partial_rows[2 * step].astype(jnp.float32) + from_left)
    returned = narrow(partial_rows[0].astype(jnp.float32) + from_right + from_left)
    grad_tokens = returned[:, :width]
    probs = returned[:, width : width + expert_count].astype(jnp.float32)
    grad_probs = narrow(jnp.sum(jnp.where(onehot, probs[:, None, :], 0.0), axis=2))

    replicas = lax.axis_size("dp")
    outer = replicas // 2
    swap = [(i, i ^ 1) for i in range(replicas)]
    xs, gs = [b[3] for b in blocks], [b[4] for b in blocks]
    pres, hiddens = [r[0] for r in results], [r[1] for r in results]
    units = down_weight.shape[1]
    chunks = [(xs, pres, 0, units), (gs, hiddens, 0, units), (xs, pres, units, units)]
    places = [0, 2, 1]
    begun = begun_weights(xs[:-4], pres[:-2], units)
    parts = weight_parts(xs[-4:], pres[-2:], 0, units, replicas, begun)
    for number, chunk in enumerate(chunks[1:], 1):
        parts += weight_parts(*chunk, replicas)
    weight_total = None
    for number, at in enumerate(places):
        sent, kept = parts[2 * number : 2 * number + 2]
        arrived = lax.ppermute(sent, "dp", swap)
        pieces = [kept, arrived]
        for shift in range(1, outer):
            pairs = [
                (2 * y + c, 2 * ((y + shift) % outer) + c) for y in range(outer) for c in range(2)
            ]
            both = kept[shift - 1].astype(jnp.float32) + arrived[shift - 1].astype(jnp.float32)
            pieces.append(lax.ppermute(narrow(both)[None], "dp", pairs))
        weight_total = place_chunk(pieces, at, local_experts, 3 * units, weight_total)
    return (grad_tokens, grad_probs, weight_total)


def solution(mesh):
    in_specs = (
        P(("dp", "expert"), None),
        P(("dp", "expert"), None),
        P(("dp", "expert"), None),
        P(("dp", "expert"), None),
        P("expert", None, None),
        P("expert", None, None),
    )
    out_specs = (P(("dp", "expert"), None), P(("dp", "expert"), None), P("dp", "expert", None))
    return jax.shard_map(layer, mesh=mesh, in_specs=in_specs, out_specs=out_specs, check_vma=False)
```

```python
import functools

import jax
import jax.numpy as jnp
from jax import lax
from jax.experimental import pallas as pl
from jax.experimental.pallas import tpu as pltpu
from jax.sharding import PartitionSpec as P


VMEM_BYTES = 67043328


def ring_order(size):
    half = size // 2
    return [2 * p if p < half else 2 * (size - 1 - p) + 1 for p in range(size)]


def joined(refs):
    parts = [ref[...] for ref in refs]
    return parts[0] if len(parts) == 1 else jnp.concatenate(parts, axis=0)


def expert_kernel(count, size, scalars, *refs):
    g_refs, gate_refs = refs[:count], refs[count : 2 * count]
    first, (w_in, w_out, pre_ref, hidden_ref) = 2 * count, refs[-(count + 5) : -(count + 1)]
    row_refs, total = refs[-(count + 1) : -1], refs[-1]
    e, last = pl.program_id(0), pl.num_programs(0) - 1
    units, width = w_out.shape[1:]
    x_refs = refs[first : -(count + 5)]
    pre = jnp.dot(joined(x_refs), w_in[0], preferred_element_type=jnp.float32)
    back = lax.dot_general(
        joined(g_refs), w_out[0], (((1,), (1,)), ((), ())), preferred_element_type=jnp.float32
    )
    gates = [ref[0].astype(jnp.float32) for ref in gate_refs]
    gates = gates[0] if count == 1 else jnp.concatenate(gates, axis=0)
    column = lax.broadcasted_iota(jnp.int32, gates.shape, 1) == e
    weight = jnp.sum(jnp.where(column, gates, 0.0), axis=1, keepdims=True)
    gate_pre, up_pre = pre[:, :units], pre[:, units:]
    logistic = 1.0 / (1.0 + jnp.exp(-gate_pre))
    active = gate_pre * logistic
    slope = logistic * (1.0 + gate_pre * (1.0 - logistic))
    hidden = (active * up_pre).astype(jnp.bfloat16).astype(jnp.float32)
    probs = jnp.sum(hidden * back, axis=1, keepdims=True)
    hidden_ref[0] = (weight * hidden).astype(jnp.bfloat16)
    grad_hidden = weight * back
    pre_ref[0, :, :units] = (grad_hidden * up_pre * slope).astype(jnp.bfloat16)
    pre_ref[0, :, units:] = (grad_hidden * active).astype(jnp.bfloat16)
    rows = lax.dot_general(
        pre_ref[0], w_in[0], (((1,), (1,)), ((), ())), preferred_element_type=jnp.float32
    )
    lane = lax.broadcasted_iota(jnp.int32, (rows.shape[0], total.shape[1] - width), 1)
    tail = jnp.where(lane == scalars[size] * pl.num_programs(0) + e, probs, 0.0)

    @pl.when(e == 0)
    def _():
        total[:, :width] = rows
        total[:, width:] = tail

    @pl.when(e > 0)
    def _():
        total[:, :width] += rows
        total[:, width:] += tail

    @pl.when(e == last)
    def _():
        at = 0
        for ref in row_refs:
            ref[...] = total[at : at + ref.shape[0]].astype(jnp.bfloat16)
            at += ref.shape[0]


def expert_blocks(blocks, table, gates, weight_in, weight_out, vmem):
    count = len(blocks)
    experts, width, wide = weight_in.shape
    units = weight_out.shape[1]
    sizes = [b[2] - b[1] for b in blocks]
    rows = sum(sizes)
    full = width + -(-gates.shape[0] * experts // 128) * 128
    whole = lambda n, w=width: pl.BlockSpec((n, w), lambda e, s: (0, 0))

    def gate_spec(offset, lo, n):
        return pl.BlockSpec((1, n, experts), lambda e, s: (s[offset], lo // n, 0))

    per_expert = lambda a, b: pl.BlockSpec((1, a, b), lambda e, s: (e, 0, 0))
    out = pl.pallas_call(
        functools.partial(expert_kernel, count, gates.shape[0]),
        out_shape=[
            jax.ShapeDtypeStruct((experts, rows, wide), jnp.bfloat16),
            jax.ShapeDtypeStruct((experts, rows, units), jnp.bfloat16),
        ]
        + [jax.ShapeDtypeStruct((n, full), jnp.bfloat16) for n in sizes],
        grid_spec=pltpu.PrefetchScalarGridSpec(
            num_scalar_prefetch=1,
            grid=(experts,),
            in_specs=[whole(n) for n in sizes]
            + [gate_spec(b[0], b[1], b[2] - b[1]) for b in blocks]
            + [whole(n) for n in sizes]
            + [per_expert(width, wide), per_expert(units, width)],
            out_specs=[per_expert(rows, wide), per_expert(rows, units)]
            + [whole(n, full) for n in sizes],
            scratch_shapes=[pltpu.VMEM((rows, full), jnp.float32)],
        ),
        cost_estimate=pl.CostEstimate(
            flops=2 * rows * experts * width * (2 * wide + units),
            bytes_accessed=2 * experts * width * (wide + units) + 8 * rows * width,
            transcendentals=0,
        ),
        compiler_params=pltpu.CompilerParams(vmem_limit_bytes=vmem),
        name="experts",
    )(table, *[b[4] for b in blocks], *[gates] * count, *[b[3] for b in blocks], weight_in, weight_out)
    return out[0], out[1], out[2:]


def begun_kernel(nx, *refs):
    p_refs = refs[nx:-1]
    experts = p_refs[0].shape[0]
    right = [jnp.concatenate([ref[e] for ref in p_refs], axis=0) for e in range(experts)]
    refs[-1][...] = lax.dot_general(
        joined(refs[:nx]),
        jnp.concatenate(right, axis=1),
        (((0,), (0,)), ((), ())),
        preferred_element_type=jnp.float32,
    ).astype(jnp.bfloat16)


def begun_weights(xs, ps, size):
    width, experts = xs[0].shape[1], ps[0].shape[0]
    depth, columns = width // 4, experts * size
    rows = sum(x.shape[0] for x in xs)
    return pl.pallas_call(
        functools.partial(begun_kernel, len(xs)),
        out_shape=jax.ShapeDtypeStruct((width, columns), jnp.bfloat16),
        grid=(width // depth,),
        in_specs=[pl.BlockSpec((x.shape[0], depth), lambda i: (0, i)) for x in xs]
        + [pl.BlockSpec((experts, p.shape[1], size), lambda i: (0, 0, 0)) for p in ps],
        out_specs=pl.BlockSpec((depth, columns), lambda i: (i, 0)),
        cost_estimate=pl.CostEstimate(
            flops=2 * rows * width * columns,
            bytes_accessed=2 * (rows * (width + columns) + width * columns),
            transcendentals=0,
        ),
        name="begun",
    )(*xs, *ps)


def weight_kernel(x_rows, p_rows, start, depth, begun_count, *refs):
    x_refs, p_refs = refs[: len(x_rows)], refs[len(x_rows) : len(x_rows) + len(p_rows)]
    begun = refs[len(x_rows) + len(p_rows) :][:begun_count]
    refs = refs[len(x_rows) + len(p_rows) + begun_count :]
    sent, kept, held, gradients, result, x_sems, p_sems, sems = refs[:8]
    outer, experts = sent.shape[0], p_refs[0].shape[0]
    size = sent.shape[2] // experts

    core, mine = lax.axis_index("dp") & 1, lax.axis_index("dp") >> 1

    def slabs(i):
        for place in range(outer):
            block = 2 * lax.rem(mine + 1 + place, outer) + (1 - core if i == 0 else core)
            column = pl.multiple_of(block * depth, depth)
            row = 0
            for k, n in enumerate(x_rows):
                yield pltpu.make_async_copy(
                    x_refs[k].at[:, pl.ds(column, depth)],
                    held.at[i, row : row + n, place * depth : (place + 1) * depth],
                    x_sems.at[i, place, k],
                )
                row += n
            for ref in begun:
                yield pltpu.make_async_copy(
                    ref.at[pl.ds(column, depth), :], refs[8].at[i, place], refs[9].at[i, place]
                )

    def gradient_copies():
        row = 0
        for k, n in enumerate(p_rows):
            for e in range(experts):
                yield pltpu.make_async_copy(
                    p_refs[k].at[e, :, start : start + size],
                    gradients.at[row : row + n, e * size : (e + 1) * size],
                    p_sems.at[k, e],
                )
            row += n

    for copy in [*slabs(0), *gradient_copies(), *slabs(1)]:
        copy.start()
    for copy in gradient_copies():
        copy.wait()
    stores = []
    for i, out in enumerate((sent, kept)):
        for copy in slabs(i):
            copy.wait()
        part = lax.dot_general(
            held[i], gradients[...], (((0,), (0,)), ((), ())), preferred_element_type=jnp.float32
        )
        part = part.reshape(result.shape[1:])
        if begun:
            part += refs[8][i].astype(jnp.float32)
        result[i] = part.astype(jnp.bfloat16)
        stores.append(pltpu.make_async_copy(result.at[i], out, sems.at[i]))
        stores[-1].start()
    for store in stores:
        store.wait()


def weight_parts(xs, ps, start, size, replicas, *begun):
    width = xs[0].shape[1]
    experts = ps[0].shape[0]
    outer, depth = replicas // 2, width // replicas
    x_rows, p_rows = [x.shape[0] for x in xs], [p.shape[1] for p in ps]
    rows, columns = sum(x_rows), experts * size

    anywhere = pl.BlockSpec(memory_space=pl.ANY)
    return pl.pallas_call(
        functools.partial(weight_kernel, x_rows, p_rows, start, depth, len(begun)),
        out_shape=[jax.ShapeDtypeStruct((outer, depth, columns), jnp.bfloat16)] * 2,
        in_specs=[anywhere] * (len(xs) + len(ps) + len(begun)),
        out_specs=[anywhere] * 2,
        scratch_shapes=[
            pltpu.VMEM((2, rows, outer * depth), jnp.bfloat16),
            pltpu.VMEM((rows, columns), jnp.bfloat16),
            pltpu.VMEM((2, outer, depth, columns), jnp.bfloat16),
            pltpu.SemaphoreType.DMA((2, outer, len(xs))),
            pltpu.SemaphoreType.DMA((len(ps), experts)),
            pltpu.SemaphoreType.DMA((2,)),
        ]
        + [
            pltpu.VMEM((2, outer, depth, columns), jnp.bfloat16),
            pltpu.SemaphoreType.DMA((2, outer)),
        ]
        * len(begun),
        cost_estimate=pl.CostEstimate(
            flops=2 * rows * width * columns,
            bytes_accessed=2 * (rows * (width + columns) + width * columns),
            transcendentals=0,
        ),
        name="weights",
    )(*xs, *ps, *begun)


def place_kernel(count, *refs):
    total = refs[0][...].astype(jnp.float32)
    for ref in refs[1:count]:
        total += ref[...].astype(jnp.float32)
    out = refs[-1]
    size = out.shape[2]
    for e in range(out.shape[1]):
        out[:, e, :] = total[:, e * size : (e + 1) * size].astype(jnp.bfloat16)


def place_chunk(pieces, at, experts, columns, held=None):
    depth, size = pieces[0].shape[1], pieces[0].shape[2] // experts
    tile = depth
    specs = [
        pl.BlockSpec((None, tile, experts * size), lambda i, last=p.shape[0] - 1: (last, i, 0))
        for p in pieces
    ]
    args = list(pieces) + ([] if held is None else [held])
    return pl.pallas_call(
        functools.partial(place_kernel, len(pieces)),
        out_shape=jax.ShapeDtypeStruct((depth, experts, columns), jnp.bfloat16),
        grid=(depth // tile,),
        in_specs=specs
        + ([] if held is None else [pl.BlockSpec(memory_space=pl.ANY)]),
        out_specs=pl.BlockSpec((tile, experts, size), lambda i: (i, 0, at)),
        input_output_aliases={} if held is None else {len(pieces): 0},
        compiler_params=pltpu.CompilerParams(vmem_limit_bytes=VMEM_BYTES),
        name="place",
    )(*args)


def layer(tokens, out_grad, expert_ids, gate_probs, gate_up_weight, down_weight):
    rows, width = tokens.shape
    local_experts = gate_up_weight.shape[0]
    size = lax.axis_size("expert")
    expert_count = local_experts * size
    half, mid = size // 2, rows // 2
    order = ring_order(size)
    forward = [(order[p], order[(p + 1) % size]) for p in range(size)]
    backward = [(b, a) for a, b in forward]
    me = lax.axis_index("expert")
    experts = jnp.arange(expert_count, dtype=jnp.int32)
    onehot = expert_ids[:, :, None] == experts[None, None, :]
    dense_gates = jnp.sum(
        jnp.where(onehot, gate_probs[:, :, None].astype(jnp.float32), 0.0), axis=1
    ).astype(jnp.bfloat16)
    gates = lax.all_to_all(dense_gates, "expert", split_axis=1, concat_axis=0, tiled=True)
    gates = gates.reshape(size, rows, local_experts)
    followers = [[order[(order.index(e) + k) % size] for k in range(size)] for e in range(size)]
    mine = lax.broadcasted_iota(jnp.int32, (size, size), 0) == me
    table = jnp.sum(jnp.where(mine, jnp.asarray(followers, jnp.int32), 0), axis=0)
    table = jnp.concatenate([table, me[None].astype(jnp.int32)])

    blocks = [(0, 0, rows, tokens, out_grad)]
    left, right = (tokens, out_grad), (tokens, out_grad)
    for step in range(1, half + 1):
        if step == half:
            left, right = tuple(a[:mid] for a in left), tuple(a[mid:] for a in right)
        xl = lax.ppermute(left[0], "expert", forward)
        xr = lax.ppermute(right[0], "expert", backward)
        left = (xl, lax.ppermute(left[1], "expert", forward))
        right = (xr, lax.ppermute(right[1], "expert", backward))
        if step < half:
            blocks.append((size - step, 0, rows) + left)
            blocks.append((step, 0, rows) + right)
    blocks.append((half, 0, mid) + left)
    blocks.append((half, mid, rows) + right)

    groups = [blocks[:3]] + [blocks[i : i + 2] for i in range(3, len(blocks), 2)]
    results = []
    for number, group in enumerate(groups):
        results.append(
            expert_blocks(
                group, table, gates, gate_up_weight, down_weight,
                {half - 1: VMEM_BYTES, half - 2: VMEM_BYTES * 14 // 15}.get(number),
            )
        )
    partial_rows = [r for result in results for r in result[2]]

    narrow = lambda a: a.astype(jnp.bfloat16)
    to_left, to_right = partial_rows[-2], partial_rows[-1]
    for step in range(half - 1, -1, -1):
        from_right = lax.ppermute(to_left, "expert", backward).astype(jnp.float32)
        from_left = lax.ppermute(to_right, "expert", forward).astype(jnp.float32)
        if step == half - 1:
            pad = jnp.zeros((mid, from_left.shape[1]), jnp.float32)
            from_right = jnp.concatenate([from_right, pad])
            from_left = jnp.concatenate([pad, from_left])
        if step > 0:
            to_left = narrow(partial_rows[2 * step - 1].astype(jnp.float32) + from_right)
            to_right = narrow(partial_rows[2 * step].astype(jnp.float32) + from_left)
    returned = narrow(partial_rows[0].astype(jnp.float32) + from_right + from_left)
    grad_tokens = returned[:, :width]
    probs = returned[:, width : width + expert_count].astype(jnp.float32)
    grad_probs = narrow(jnp.sum(jnp.where(onehot, probs[:, None, :], 0.0), axis=2))

    replicas = lax.axis_size("dp")
    outer = replicas // 2
    swap = [(i, i ^ 1) for i in range(replicas)]
    xs, gs = [b[3] for b in blocks], [b[4] for b in blocks]
    pres, hiddens = [r[0] for r in results], [r[1] for r in results]
    units = down_weight.shape[1]
    chunks = [(xs, pres, 0, units), (gs, hiddens, 0, units), (xs, pres, units, units)]
    places = [0, 2, 1]
    begun = begun_weights(xs[:-4], pres[:-2], units)
    parts = weight_parts(xs[-4:], pres[-2:], 0, units, replicas, begun)
    for number, chunk in enumerate(chunks[1:], 1):
        parts += weight_parts(*chunk, replicas)
    weight_total = None
    for number, at in enumerate(places):
        sent, kept = parts[2 * number : 2 * number + 2]
        arrived = lax.ppermute(sent, "dp", swap)
        crossed = []
        for shift in range(1, outer):
            pairs = [
                (2 * y + c, 2 * ((y + shift) % outer) + c) for y in range(outer) for c in range(2)
            ]
            both = kept[shift - 1].astype(jnp.float32) + arrived[shift - 1].astype(jnp.float32)
            crossed.append(lax.ppermute(narrow(both)[None], "dp", pairs))
        own = narrow(kept[-1].astype(jnp.float32) + arrived[-1].astype(jnp.float32))[None]
        pieces = [own, *crossed]
        weight_total = place_chunk(pieces, at, local_experts, 3 * units, weight_total)
    return (grad_tokens, grad_probs, weight_total)


def solution(mesh):
    in_specs = (
        P(("dp", "expert"), None),
        P(("dp", "expert"), None),
        P(("dp", "expert"), None),
        P(("dp", "expert"), None),
        P("expert", None, None),
        P("expert", None, None),
    )
    out_specs = (P(("dp", "expert"), None), P(("dp", "expert"), None), P("dp", "expert", None))
    return jax.shard_map(layer, mesh=mesh, in_specs=in_specs, out_specs=out_specs, check_vma=False)
```
